32 devices in a mesh: src: 4 (over z), tm: 8 (over y, x, core).
Axes of the slice: x: 2, y: 2, z: 4, core: 2. Of those that a mesh axis runs over, the one named last changes fastest.
Arguments:
- greens: bfloat16 [16384, 3072], P('tm', 'src')
- pairs: int32 [4, 2], P('src'), may hold values from 0 to 3, as said below
- onsets: int32 [4], replicated, may hold values from 0 to 8191
Outputs:
- gram: float32 [4, 768, 768], P('src', 'tm')
The draws below stay inside these ranges and needn't reach their ends.
Inputs may be any that keep to these rules, and one draw needn't show every extreme that they name: `pairs`: row s names the blocks s and (s - 1) mod 4, in either order.
All inputs are finite; a program needn't handle non-finite values.
Results may differ from the reference program's by a relative error of at most 0.0003.
Values may be sent and summed in bfloat16 or wider, within the bound.
No kernel may reach another device: no remote copies, remote signals or barrier semaphores. Data moves between devices by JAX's collectives and lax.ppermute only.
A program may use at most 64 MiB of HBM per device.

```python
import jax
import jax.numpy as jnp
from jax import lax

SRC_BLK = 768
BLOCKS = 4
ROWS = 16384


def draw_greens(key, part):
    factors = 16
    base_key = jax.random.fold_in(key, 11)
    keys = jax.random.split(base_key, 4)
    basis = jax.random.normal(keys[0], (ROWS, factors), jnp.float32)
    centres = jax.random.uniform(keys[1], (factors,), jnp.float32) * ROWS
    row_pos = jnp.arange(ROWS, dtype=jnp.float32)
    envelope = jnp.exp(-((row_pos[:, None] - centres[None, :]) / (0.3 * ROWS)) ** 2)
    rising = 1.0 + 0.8 * row_pos / ROWS
    shaped = basis * envelope

    def one_block(index):
        block_key = jax.random.fold_in(keys[3], index)
        mix_key, noise_key = jax.random.split(block_key, 2)
        mix = jax.random.normal(mix_key, (factors, SRC_BLK), jnp.float32) * 0.35
        noise = jax.random.normal(noise_key, (ROWS, SRC_BLK), jnp.float32)
        values = jnp.dot(shaped, mix, precision=lax.Precision.HIGHEST) + noise
        values = values * rising[:, None] * 0.6
        return values.astype(jnp.bfloat16)
    blocks = lax.map(one_block, jnp.arange(BLOCKS, dtype=jnp.int32))
    return jnp.moveaxis(blocks, 0, 1).reshape(ROWS, BLOCKS * SRC_BLK)


def draw_pairs(key, part):
    owners = jnp.arange(BLOCKS, dtype=jnp.int32)
    before = (owners + BLOCKS - 1) % BLOCKS
    flips = jax.random.randint(jax.random.fold_in(key, 23), (BLOCKS,), 0, 2, dtype=jnp.int32)
    first = jnp.where(flips == 1, owners, before)
    second = jnp.where(flips == 1, before, owners)
    return jnp.stack([first, second], axis=1).astype(jnp.int32)


def with_ends(values, own_key, least, high):
    longest = values.shape.index(max(values.shape))
    spots = []
    for shift in (0, 1):
        where = [jax.random.randint(jax.random.fold_in(own_key, axis), (), 0, length) for axis, length in enumerate(values.shape)]
        where[longest] = (where[longest] + shift) % values.shape[longest]
        spots.append(tuple(where))
    return values.at[spots[0]].set(least).at[spots[1]].set(high)


def setup_inputs(seed: int = 0) -> dict:
    streams_of = jax.random.split(jax.random.key(seed), 4)
    greens = draw_greens(jax.random.fold_in(streams_of[3], 71), 0)
    pairs = draw_pairs(jax.random.fold_in(streams_of[3], 71), 0)
    onsets = with_ends(jax.random.randint(streams_of[2], (BLOCKS,), 0, ROWS // 2), jax.random.fold_in(streams_of[2], 1), 0, (ROWS // 2) - 1).astype(jnp.int32)
    return dict(greens=greens, pairs=pairs, onsets=onsets)


def masked_block(greens, block, onset):
    piece = lax.dynamic_slice(greens, (jnp.int32(0), (block * SRC_BLK).astype(jnp.int32)), (ROWS, SRC_BLK))
    row_ids = jnp.arange(ROWS, dtype=jnp.int32)
    return jnp.where((row_ids >= onset)[:, None], piece, jnp.zeros_like(piece))

def reference(greens, pairs, onsets):

    def one_tile(pair):
        first = pair[0]
        second = pair[1]
        left = masked_block(greens, first, onsets[first])
        right = masked_block(greens, second, onsets[second])
        left_f = left.astype(jnp.float32)
        right_f = right.astype(jnp.float32)
        norm_left = lax.optimization_barrier(jnp.sum(left_f * left_f, axis=0))
        norm_right = lax.optimization_barrier(jnp.sum(right_f * right_f, axis=0))
        product = lax.dot_general(left, right, (((0,), (0,)), ((), ())), preferred_element_type=jnp.float32)
        return product * lax.rsqrt(norm_left + 1e-06)[:, None] * lax.rsqrt(norm_right + 1e-06)[None, :]
    return lax.map(one_tile, pairs)
```

```python
import jax
import jax.numpy as jnp
from jax import lax
from jax.sharding import PartitionSpec as P


def from_behind(value, axis, by):
    length = lax.axis_size(axis)
    return lax.ppermute(value, axis, [(i, (i + by) % length) for i in range(length)])


def swapped(value, axis, bits):
    length = lax.axis_size(axis)
    return lax.ppermute(value, axis, [(i, i ^ bits) for i in range(length)])


def summed(value, axis):
    bits = 1
    while bits < lax.axis_size(axis):
        value = value + swapped(value, axis, bits)
        bits *= 2
    return value


def strips_summed(tile, axis):
    length = lax.axis_size(axis)
    me = lax.axis_index(axis)
    height, width = tile.shape
    strips = tile.reshape(length // 2, 2, height // length, width)
    bit = me % 2
    pair = me // 2
    keep = lax.dynamic_index_in_dim(strips, bit, 1, keepdims=False)
    give = lax.dynamic_index_in_dim(strips, 1 - bit, 1, keepdims=False)
    half = keep + swapped(give, axis, 1)
    arrived = [
        swapped(lax.dynamic_index_in_dim(half, pair ^ m, 0, keepdims=False), axis, 2 * m)
        for m in range(1, length // 2)
    ]
    mine = lax.dynamic_index_in_dim(half, pair, 0, keepdims=False)
    for strip in arrived:
        mine = mine + strip
    return mine


def on_device(greens, pairs, onsets):
    rows_dev, width = greens.shape
    row_group = lax.axis_index("tm")
    row_start = row_group * rows_dev
    owner = lax.axis_index("src")
    blocks = lax.axis_size("src")
    lower = from_behind(greens, "src", 1)
    owner_first = pairs[0, 0] == owner
    own_onset = onsets[owner]
    arrival = jnp.maximum(own_onset, onsets[(owner + blocks - 1) % blocks])
    row_ids = row_start + jnp.arange(rows_dev, dtype=jnp.int32)
    own_f = jnp.where((row_ids >= own_onset)[:, None], greens.astype(jnp.float32), 0.0)
    norm_own = summed(jnp.sum(own_f * own_f, axis=0), "tm")
    norm_low = from_behind(norm_own, "src", 1)
    own = jnp.where((row_ids >= arrival)[:, None], greens, jnp.zeros_like(greens))
    own, norm_own, norm_low = lax.optimization_barrier((own, norm_own, norm_low))

    def product(a, b):
        return lax.dot_general(
            a, b, (((0,), (0,)), ((), ())), preferred_element_type=jnp.float32
        )

    silent = row_start + rows_dev <= arrival
    case = jnp.where(silent, 0, jnp.where(owner_first, 1, 2))
    tile = lax.switch(
        case,
        [
            lambda a, b: jnp.zeros((width, width), jnp.float32),
            lambda a, b: product(a, b),
            lambda a, b: product(b, a),
        ],
        own,
        lower,
    )
    scale_own = lax.rsqrt(norm_own + 1e-06)
    scale_low = lax.rsqrt(norm_low + 1e-06)
    share = width // lax.axis_size("tm")
    scale_rows = lax.dynamic_slice_in_dim(
        jnp.where(owner_first, scale_own, scale_low), row_group * share, share, 0
    )
    scale_cols = jnp.where(owner_first, scale_low, scale_own)
    mine = strips_summed(tile, "tm")
    return (mine * scale_rows[:, None] * scale_cols[None, :])[None]


def solution(mesh):
    in_specs = (P("tm", "src"), P("src", None), P())
    out_specs = P("src", "tm", None)
    return jax.shard_map(
        on_device, mesh=mesh, in_specs=in_specs, out_specs=out_specs, check_vma=False
    )
```

```python
import functools

import jax
import jax.numpy as jnp
from jax import lax
from jax.experimental import pallas as pl
from jax.experimental.pallas import tpu as pltpu
from jax.sharding import PartitionSpec as P


PARTS = (2, 2, 1, 1)
HEAD = 8


def from_behind(value, axis, by):
    length = lax.axis_size(axis)
    return lax.ppermute(value, axis, [(i, (i + by) % length) for i in range(length)])


def swapped(value, axis, bits):
    length = lax.axis_size(axis)
    return lax.ppermute(value, axis, [(i, i ^ bits) for i in range(length)])


def summed(value, axis):
    bits = 1
    while bits < lax.axis_size(axis):
        value = value + swapped(value, axis, bits)
        bits *= 2
    return value


def split(strips, bit):
    halves = strips.reshape((strips.shape[0] // 2, 2) + strips.shape[1:])
    keep = lax.dynamic_index_in_dim(halves, bit, 1, keepdims=False)
    give = lax.dynamic_index_in_dim(halves, 1 - bit, 1, keepdims=False)
    return keep, give


def strips_arrived(keep, give, axis):
    me = lax.axis_index(axis) // 2
    bits = 1
    strips = keep + swapped(give, axis, bits)
    while strips.shape[0] > 4:
        keep, give = split(strips, me % 2)
        bits *= 2
        me = me // 2
        strips = keep + swapped(give, axis, bits)
    bits *= 2
    terms = [lax.dynamic_index_in_dim(strips, me, 0, keepdims=False)]
    for m in range(1, strips.shape[0]):
        give = lax.dynamic_index_in_dim(strips, me ^ m, 0, keepdims=False)
        terms.append(swapped(give, axis, bits * m))
    return terms


def runs_of(share):
    whole = sum(PARTS)
    if share % whole:
        return [(0, share)]
    unit = share // whole
    runs, start = [], 0
    for part in PARTS:
        runs.append((start, part * unit))
        start += part * unit
    return runs


def picker(width, share, start, run):
    picked = width // share * run
    q = lax.broadcasted_iota(jnp.int32, (width, picked), 1)
    source = lax.broadcasted_iota(jnp.int32, (width, picked), 0)
    return (q // run) * share + start + q % run == source


def picked(block, share, start, run):
    return jnp.dot(
        block,
        picker(block.shape[1], share, start, run).astype(jnp.bfloat16),
        preferred_element_type=jnp.float32,
    ).astype(jnp.bfloat16)


def gram_kernel(lane, share, run, flags, own, head, rest, keep, give, part):
    cut = head.shape[0]
    columns = rest.shape[1]
    groups = keep.shape[0] * 2
    bit = flags[1]
    product = jnp.dot(
        own[:, cut:], rest[...], preferred_element_type=jnp.float32
    ) + jnp.dot(
        own[:, :cut], head[:, lane : lane + columns], preferred_element_type=jnp.float32
    )

    @pl.when(flags[0] == 1)
    def _():
        part[...] = product
        for pair in range(groups // 2):
            for target, odd in ((keep, bit), (give, 1 - bit)):
                top = (2 * pair + odd) * share
                for piece in range(share // run):
                    rows = pl.ds(pl.multiple_of(top + piece * run, 8), run)
                    target[pair, :, piece * columns : (piece + 1) * columns] = part[rows, :]

    @pl.when(flags[0] == 0)
    def _():
        turned = product.T
        for pair in range(groups // 2):
            even = turned[2 * pair * run : (2 * pair + 1) * run, :]
            uneven = turned[(2 * pair + 1) * run : (2 * pair + 2) * run, :]
            keep[pair] = jnp.where(bit == 0, even, uneven)
            give[pair] = jnp.where(bit == 0, uneven, even)


def gram(flags, own, head, rest, share, start, run):
    width = own.shape[0]
    groups = width // share
    half = jax.ShapeDtypeStruct((groups // 2, run, width), jnp.float32)
    columns = groups * run
    return pl.pallas_call(
        functools.partial(gram_kernel, start * groups, share, run),
        out_shape=(half, half),
        in_specs=[pl.BlockSpec(memory_space=pltpu.SMEM)]
        + [pl.BlockSpec(memory_space=pltpu.VMEM)] * 3,
        out_specs=(pl.BlockSpec(memory_space=pltpu.VMEM),) * 2,
        scratch_shapes=[pltpu.VMEM((width, columns), jnp.float32)],
        cost_estimate=pl.CostEstimate(
            flops=2 * own.size * columns, bytes_accessed=2 * own.size, transcendentals=0
        ),
        compiler_params=pltpu.CompilerParams(vmem_limit_bytes=16 << 20),
        name="gram",
    )(flags, own, head, rest)


def gram_plain(flags, own, head, rest, share, start, run):
    width = own.shape[0]
    groups = width // share
    columns = groups * run
    block = jnp.concatenate([head[:, start * groups : start * groups + columns], rest], axis=0)
    product = jnp.dot(own, block, preferred_element_type=jnp.float32)
    strips = jnp.where(
        flags[0] == 1,
        product.reshape(groups, share // run, run, columns)
        .transpose(0, 2, 1, 3)
        .reshape(groups, run, width),
        product.T.reshape(groups, run, width),
    )
    return split(strips, flags[1])


def put_back(runs, share, parts):
    width = parts[0].shape[1]
    total = jnp.zeros((share, width), jnp.float32)
    for (start, run), part in zip(runs, parts):
        columns = width // share * run
        spread = (
            part.reshape(run, share // run, columns).transpose(1, 0, 2).reshape(share, columns)
        )
        total = total + lax.dot_general(
            spread,
            picker(width, share, start, run).astype(jnp.float32),
            (((1,), (1,)), ((), ())),
            precision=lax.Precision.HIGHEST,
            preferred_element_type=jnp.float32,
        )
    return total


def finish_kernel(share, start, run, flags, base, scale_rows, scale_cols, *refs):
    *terms, out = refs
    width = base.shape[1]
    columns = width // share * run
    part = terms[0][...]
    for term in terms[1:]:
        part = part + term[...]

    @pl.when(flags[0] == 1)
    def _():
        spread = jnp.concatenate(
            [part[:, n * columns : (n + 1) * columns] for n in range(share // run)], axis=0
        )
        q = lax.broadcasted_iota(jnp.int32, (columns, width), 0)
        source = lax.broadcasted_iota(jnp.int32, (columns, width), 1)
        order = (q // run) * share + start + q % run == source
        placed = jnp.dot(
            spread,
            order.astype(jnp.float32),
            precision=lax.Precision.HIGHEST,
            preferred_element_type=jnp.float32,
        )
        out[0] = (base[...] + placed) * scale_rows[...] * scale_cols[...]

    @pl.when(flags[0] == 0)
    def _():
        out[0] = base[...] * scale_rows[...] * scale_cols[...]
        out[0, start : start + run, :] = (
            part * scale_rows[start : start + run, :] * scale_cols[...]
        )


def finish(flags, base, scale_rows, scale_cols, terms, share, start, run):
    return pl.pallas_call(
        functools.partial(finish_kernel, share, start, run),
        out_shape=jax.ShapeDtypeStruct((1,) + base.shape, jnp.float32),
        in_specs=[pl.BlockSpec(memory_space=pltpu.SMEM)]
        + [pl.BlockSpec(memory_space=pltpu.VMEM)] * (3 + len(terms)),
        out_specs=pl.BlockSpec(memory_space=pltpu.VMEM),
        cost_estimate=pl.CostEstimate(
            flops=2 * base.size * 256, bytes_accessed=8 * base.size, transcendentals=0
        ),
        compiler_params=pltpu.CompilerParams(vmem_limit_bytes=8 << 20),
        name="finish",
    )(flags, base, scale_rows, scale_cols, *terms)


def on_device(greens, pairs, onsets):
    rows_dev, width = greens.shape
    groups = lax.axis_size("tm")
    share = width // groups
    row_group = lax.axis_index("tm")
    row_start = row_group * rows_dev
    owner = lax.axis_index("src")
    blocks = lax.axis_size("src")
    runs = runs_of(share)
    aligned = all(run % 8 == 0 and groups * run % 128 == 0 for _, run in runs)
    cut = rows_dev // HEAD

    owner_first = pairs[0, 0] == owner
    own_onset = onsets[owner]
    arrival = jnp.maximum(own_onset, onsets[(owner + blocks - 1) % blocks])
    row_ids = row_start + jnp.arange(rows_dev, dtype=jnp.int32)
    flags = jnp.stack([owner_first.astype(jnp.int32), row_group % 2])

    head = from_behind(greens[:cut], "src", 1)
    lower = []
    for run in runs:
        lower.append(from_behind(picked(greens[cut:], share, *run), "src", 1))
    own_f = jnp.where((row_ids >= own_onset)[:, None], greens.astype(jnp.float32), 0.0)
    norm_own = summed(jnp.sum(own_f * own_f, axis=0), "tm")
    norm_low = from_behind(norm_own, "src", 1)
    own = jnp.where((row_ids >= arrival)[:, None], greens, jnp.zeros_like(greens)).T
    head = jnp.concatenate([picked(head, share, *run) for run in runs], axis=1)

    done = []
    for step, (run, block) in enumerate(zip(runs, lower)):
        form = gram if aligned else gram_plain
        keep, give = form(flags, own, head, block, share, *run)
        terms = strips_arrived(keep, give, "tm")
        if step == len(runs) - 1:
            done.append(terms)
        else:
            done.append(functools.reduce(jnp.add, terms))

    scale_own = lax.rsqrt(norm_own + 1e-06)
    scale_low = lax.rsqrt(norm_low + 1e-06)
    scale_rows = lax.dynamic_slice_in_dim(
        jnp.where(owner_first, scale_own, scale_low), row_group * share, share, 0
    )[:, None]
    scale_cols = jnp.where(owner_first, scale_low, scale_own)[None, :]
    early, last = done[:-1], done[-1]
    if not aligned:
        early, last = early + [functools.reduce(jnp.add, last)], []
    base = lax.cond(
        owner_first,
        lambda *parts: put_back(runs, share, parts),
        lambda *parts: jnp.concatenate(
            parts + (jnp.zeros((share - sum(p.shape[0] for p in parts), width), jnp.float32),),
            axis=0,
        ),
        *early,
    )
    if aligned:
        return finish(flags, base, scale_rows, scale_cols, last, share, *runs[-1])
    return (base * scale_rows * scale_cols)[None]


def solution(mesh):
    in_specs = (P("tm", "src"), P("src", None), P())
    out_specs = P("src", "tm", None)
    return jax.shard_map(
        on_device, mesh=mesh, in_specs=in_specs, out_specs=out_specs, check_vma=False
    )
```

```python
import functools

import jax
import jax.numpy as jnp
from jax import lax
from jax.experimental import pallas as pl
from jax.experimental.pallas import tpu as pltpu
from jax.sharding import PartitionSpec as P


PARTS = (2, 2, 2)
HEAD = 8


def from_behind(value, axis, by):
    length = lax.axis_size(axis)
    return lax.ppermute(value, axis, [(i, (i + by) % length) for i in range(length)])


def swapped(value, axis, bits):
    length = lax.axis_size(axis)
    return lax.ppermute(value, axis, [(i, i ^ bits) for i in range(length)])


def summed(value, axis):
    bits = 1
    while bits < lax.axis_size(axis):
        value = value + swapped(value, axis, bits)
        bits *= 2
    return value


def split(strips, bit):
    halves = strips.reshape((strips.shape[0] // 2, 2) + strips.shape[1:])
    keep = lax.dynamic_index_in_dim(halves, bit, 1, keepdims=False)
    give = lax.dynamic_index_in_dim(halves, 1 - bit, 1, keepdims=False)
    return keep, give


def strips_arrived(keep, give, axis):
    me = lax.axis_index(axis) // 2
    bits = 1
    strips = keep + swapped(give, axis, bits)
    while strips.shape[0] > 4:
        keep, give = split(strips, me % 2)
        bits *= 2
        me = me // 2
        strips = keep + swapped(give, axis, bits)
    bits *= 2
    terms = [lax.dynamic_index_in_dim(strips, me, 0, keepdims=False)]
    for m in range(1, strips.shape[0]):
        give = lax.dynamic_index_in_dim(strips, me ^ m, 0, keepdims=False)
        terms.append(swapped(give, axis, bits * m))
    return terms


def runs_of(share):
    whole = sum(PARTS)
    if share % whole:
        return [(0, share)]
    unit = share // whole
    runs, start = [], 0
    for part in PARTS:
        runs.append((start, part * unit))
        start += part * unit
    return runs


def picker(width, share, start, run):
    picked = width // share * run
    q = lax.broadcasted_iota(jnp.int32, (width, picked), 1)
    source = lax.broadcasted_iota(jnp.int32, (width, picked), 0)
    return (q // run) * share + start + q % run == source


def picks_kernel(share, runs, skip, block, *outs):
    width = block.shape[1]
    source = block[skip:, :]
    for (start, run), out in zip(runs, outs):
        order = picker(width, share, start, run).astype(jnp.float32).astype(jnp.bfloat16)
        out[...] = jnp.dot(source, order, preferred_element_type=jnp.float32).astype(jnp.bfloat16)


def picks(block, share, runs, skip):
    rows, width = block.shape
    groups = width // share
    return pl.pallas_call(
        functools.partial(picks_kernel, share, runs, skip),
        out_shape=[
            jax.ShapeDtypeStruct((rows - skip, groups * run), jnp.bfloat16) for _, run in runs
        ],
        in_specs=[pl.BlockSpec(memory_space=pltpu.VMEM)],
        out_specs=[pl.BlockSpec(memory_space=pltpu.VMEM) for _ in runs],
        cost_estimate=pl.CostEstimate(
            flops=2 * block.size * width, bytes_accessed=4 * block.size, transcendentals=0
        ),
        compiler_params=pltpu.CompilerParams(vmem_limit_bytes=24 << 20),
        name="picks",
    )(block)


def turn_kernel(step, firsts, block, turned, squares):
    rows, width = block.shape
    total = jnp.zeros((1, width), jnp.float32)
    for top in range(0, rows, step):
        piece = block[top : top + step, :]
        ids = lax.broadcasted_iota(jnp.int32, (step, width), 0) + top
        wide = jnp.where(ids >= firsts[0], piece.astype(jnp.float32), 0.0)
        total = total + jnp.sum(wide * wide, axis=0, keepdims=True)
        shown = jnp.where(ids >= firsts[1], piece.astype(jnp.float32), 0.0)
        turned[:, top : top + step] = shown.T.astype(jnp.bfloat16)
    squares[...] = total


def turn(firsts, block):
    rows, width = block.shape
    step = 128 if rows % 128 == 0 else rows
    return pl.pallas_call(
        functools.partial(turn_kernel, step),
        out_shape=(
            jax.ShapeDtypeStruct((width, rows), jnp.bfloat16),
            jax.ShapeDtypeStruct((1, width), jnp.float32),
        ),
        in_specs=[pl.BlockSpec(memory_space=pltpu.SMEM), pl.BlockSpec(memory_space=pltpu.VMEM)],
        out_specs=(pl.BlockSpec(memory_space=pltpu.VMEM),) * 2,
        cost_estimate=pl.CostEstimate(
            flops=4 * block.size, bytes_accessed=4 * block.size, transcendentals=0
        ),
        compiler_params=pltpu.CompilerParams(vmem_limit_bytes=16 << 20),
        name="turn",
    )(firsts, block)


def gram_kernel(share, run, flags, own, head, rest, keep, give, part):
    cut = head.shape[0]
    columns = rest.shape[1]
    groups = keep.shape[0] * 2
    bit = flags[1]
    product = jnp.dot(
        own[:, cut:], rest[...], preferred_element_type=jnp.float32
    ) + jnp.dot(
        own[:, :cut], head[...], preferred_element_type=jnp.float32
    )

    @pl.when(flags[0] == 1)
    def _():
        part[...] = product
        for pair in range(groups // 2):
            for target, odd in ((keep, bit), (give, 1 - bit)):
                top = (2 * pair + odd) * share
                for piece in range(share // run):
                    rows = pl.ds(pl.multiple_of(top + piece * run, 8), run)
                    target[pair, :, piece * columns : (piece + 1) * columns] = part[rows, :]

    @pl.when(flags[0] == 0)
    def _():
        turned = product.T
        for pair in range(groups // 2):
            even = turned[2 * pair * run : (2 * pair + 1) * run, :]
            uneven = turned[(2 * pair + 1) * run : (2 * pair + 2) * run, :]
            keep[pair] = jnp.where(bit == 0, even, uneven)
            give[pair] = jnp.where(bit == 0, uneven, even)


def gram(flags, own, head, rest, share, run):
    width = own.shape[0]
    groups = width // share
    half = pltpu.VMEM((groups // 2, run, width), jnp.float32)
    columns = groups * run
    return pl.pallas_call(
        functools.partial(gram_kernel, share, run),
        out_shape=(half, half),
        in_specs=[pl.BlockSpec(memory_space=pltpu.SMEM)]
        + [pl.BlockSpec(memory_space=pltpu.VMEM)] * 3,
        out_specs=(pl.BlockSpec(memory_space=pltpu.VMEM),) * 2,
        scratch_shapes=[pltpu.VMEM((width, columns), jnp.float32)],
        cost_estimate=pl.CostEstimate(
            flops=2 * own.size * columns, bytes_accessed=2 * own.size, transcendentals=0
        ),
        compiler_params=pltpu.CompilerParams(vmem_limit_bytes=16 << 20),
        name="gram",
    )(flags, own, head, rest)


def gram_plain(flags, own, head, rest, share, run):
    width = own.shape[0]
    groups = width // share
    columns = groups * run
    block = jnp.concatenate([head, rest], axis=0)
    product = jnp.dot(own, block, preferred_element_type=jnp.float32)
    strips = jnp.where(
        flags[0] == 1,
        product.reshape(groups, share // run, run, columns)
        .transpose(0, 2, 1, 3)
        .reshape(groups, run, width),
        product.T.reshape(groups, run, width),
    )
    return split(strips, flags[1])


def put_back(runs, share, parts):
    width = parts[0].shape[1]
    total = jnp.zeros((share, width), jnp.float32)
    for (start, run), part in zip(runs, parts):
        columns = width // share * run
        spread = (
            part.reshape(run, share // run, columns).transpose(1, 0, 2).reshape(share, columns)
        )
        total = total + lax.dot_general(
            spread,
            picker(width, share, start, run).astype(jnp.float32),
            (((1,), (1,)), ((), ())),
            precision=lax.Precision.HIGHEST,
            preferred_element_type=jnp.float32,
        )
    return total


def placed(flags, share, start, run, part, total):
    width = total.shape[1]
    columns = width // share * run

    @pl.when(flags[0] == 1)
    def _():
        spread = jnp.concatenate(
            [part[:, n * columns : (n + 1) * columns] for n in range(share // run)], axis=0
        )
        q = lax.broadcasted_iota(jnp.int32, (columns, width), 0)
        source = lax.broadcasted_iota(jnp.int32, (columns, width), 1)
        order = (q // run) * share + start + q % run == source
        total[...] += jnp.dot(
            spread,
            order.astype(jnp.float32),
            precision=lax.Precision.HIGHEST,
            preferred_element_type=jnp.float32,
        )

    @pl.when(flags[0] == 0)
    def _():
        total[start : start + run, :] = part


def base_kernel(share, runs, flags, *refs):
    *parts, total = refs
    total[...] = jnp.zeros_like(total)
    for (start, run), part in zip(runs, parts):
        placed(flags, share, start, run, part[...], total)


def finish_kernel(share, start, run, flags, base, scale_rows, scale_cols, *refs):
    *terms, out, total = refs
    total[...] = base[...]
    part = terms[0][...]
    for term in terms[1:]:
        part = part + term[...]
    placed(flags, share, start, run, part, total)
    out[0] = total[...] * scale_rows[...] * scale_cols[...]


def base_of(flags, parts, share, runs):
    width = parts[0].shape[1]
    return pl.pallas_call(
        functools.partial(base_kernel, share, runs),
        out_shape=pltpu.VMEM((share, width), jnp.float32),
        in_specs=[pl.BlockSpec(memory_space=pltpu.SMEM)]
        + [pl.BlockSpec(memory_space=pltpu.VMEM)] * len(parts),
        out_specs=pl.BlockSpec(memory_space=pltpu.VMEM),
        cost_estimate=pl.CostEstimate(
            flops=2 * share * width * 512, bytes_accessed=8 * share * width, transcendentals=0
        ),
        compiler_params=pltpu.CompilerParams(vmem_limit_bytes=8 << 20),
        name="base",
    )(flags, *parts)


def finish(flags, base, scale_rows, scale_cols, terms, share, start, run):
    return pl.pallas_call(
        functools.partial(finish_kernel, share, start, run),
        out_shape=jax.ShapeDtypeStruct((1,) + base.shape, jnp.float32),
        in_specs=[pl.BlockSpec(memory_space=pltpu.SMEM)]
        + [pl.BlockSpec(memory_space=pltpu.VMEM)] * (3 + len(terms)),
        out_specs=pl.BlockSpec(memory_space=pltpu.VMEM),
        scratch_shapes=[pltpu.VMEM(base.shape, jnp.float32)],
        cost_estimate=pl.CostEstimate(
            flops=2 * base.size * 256, bytes_accessed=8 * base.size, transcendentals=0
        ),
        compiler_params=pltpu.CompilerParams(vmem_limit_bytes=8 << 20),
        name="finish",
    )(flags, base, scale_rows, scale_cols, *terms)


def on_device(greens, pairs, onsets):
    rows_dev, width = greens.shape
    groups = lax.axis_size("tm")
    share = width // groups
    row_group = lax.axis_index("tm")
    row_start = row_group * rows_dev
    owner = lax.axis_index("src")
    blocks = lax.axis_size("src")
    runs = runs_of(share)
    aligned = all(run % 8 == 0 and groups * run % 128 == 0 for _, run in runs)
    cut = rows_dev // HEAD

    owner_first = pairs[0, 0] == owner
    own_onset = onsets[owner]
    arrival = jnp.maximum(own_onset, onsets[(owner + blocks - 1) % blocks])
    firsts = jnp.stack([own_onset, arrival]) - row_start
    flags = jnp.stack([owner_first.astype(jnp.int32), row_group % 2])

    head = from_behind(greens[:cut], "src", 1)
    chosen = picks(greens, share, runs, cut)
    lower = []
    for block in chosen:
        lower.append(from_behind(block, "src", 1))
    own, squares = turn(firsts, greens)
    norm_own = summed(squares[0], "tm")
    norm_low = from_behind(norm_own, "src", 1)
    heads = picks(head, share, runs, 0)

    done = []
    for step, (run, top, block) in enumerate(zip(runs, heads, lower)):
        form = gram if aligned else gram_plain
        keep, give = form(flags, own, top, block, share, run[1])
        terms = strips_arrived(keep, give, "tm")
        if step == len(runs) - 1:
            done.append(terms)
        else:
            done.append(functools.reduce(jnp.add, terms))

    scale_own = lax.rsqrt(norm_own + 1e-06)
    scale_low = lax.rsqrt(norm_low + 1e-06)
    scale_rows = lax.dynamic_slice_in_dim(
        jnp.where(owner_first, scale_own, scale_low), row_group * share, share, 0
    )[:, None]
    scale_cols = jnp.where(owner_first, scale_low, scale_own)[None, :]
    if aligned:
        base = base_of(flags, done[:-1], share, runs[:-1])
        return finish(flags, base, scale_rows, scale_cols, done[-1], share, *runs[-1])
    parts = done[:-1] + [functools.reduce(jnp.add, done[-1])]
    base = jnp.where(
        owner_first, put_back(runs, share, parts), jnp.concatenate(parts, axis=0)
    )
    return (base * scale_rows * scale_cols)[None]


def solution(mesh):
    in_specs = (P("tm", "src"), P("src", None), P())
    out_specs = P("src", "tm", None)
    return jax.shard_map(
        on_device, mesh=mesh, in_specs=in_specs, out_specs=out_specs, check_vma=False
    )
```

```python
import functools

import jax
import jax.numpy as jnp
from jax import lax
from jax.experimental import pallas as pl
from jax.experimental.pallas import tpu as pltpu
from jax.sharding import PartitionSpec as P


PARTS = (2, 2, 2)
HEAD = 8


def from_behind(value, axis, by):
    length = lax.axis_size(axis)
    return lax.ppermute(value, axis, [(i, (i + by) % length) for i in range(length)])


def swapped(value, axis, bits):
    length = lax.axis_size(axis)
    return lax.ppermute(value, axis, [(i, i ^ bits) for i in range(length)])


def summed(value, axis):
    bits = 1
    while bits < lax.axis_size(axis):
        value = plus(value, swapped(value, axis, bits))
        bits *= 2
    return value


def split(strips, bit):
    halves = strips.reshape((strips.shape[0] // 2, 2) + strips.shape[1:])
    keep = lax.dynamic_index_in_dim(halves, bit, 1, keepdims=False)
    give = lax.dynamic_index_in_dim(halves, 1 - bit, 1, keepdims=False)
    return keep, give


def strips_arrived(keep, give, axis):
    me = lax.axis_index(axis) // 2
    bits = 1
    strips = keep + swapped(give, axis, bits)
    while strips.shape[0] > 4:
        keep, give = split(strips, me % 2)
        bits *= 2
        me = me // 2
        strips = keep + swapped(give, axis, bits)
    bits *= 2
    terms = [lax.dynamic_index_in_dim(strips, me, 0, keepdims=False)]
    for m in range(1, strips.shape[0]):
        give = lax.dynamic_index_in_dim(strips, me ^ m, 0, keepdims=False)
        terms.append(swapped(give, axis, bits * m))
    return terms


def runs_of(share):
    whole = sum(PARTS)
    if share % whole:
        return [(0, share)]
    unit = share // whole
    runs, start = [], 0
    for part in PARTS:
        runs.append((start, part * unit))
        start += part * unit
    return runs


def picker(width, share, start, run):
    picked = width // share * run
    q = lax.broadcasted_iota(jnp.int32, (width, picked), 1)
    source = lax.broadcasted_iota(jnp.int32, (width, picked), 0)
    return (q // run) * share + start + q % run == source


def picks_kernel(share, runs, skip, block, *outs):
    width = block.shape[1]
    source = block[skip:, :]
    for (start, run), out in zip(runs, outs):
        order = picker(width, share, start, run).astype(jnp.float32).astype(jnp.bfloat16)
        out[...] = jnp.dot(source, order, preferred_element_type=jnp.float32).astype(jnp.bfloat16)


def picks(block, share, runs, skip):
    rows, width = block.shape
    groups = width // share
    return pl.pallas_call(
        functools.partial(picks_kernel, share, runs, skip),
        out_shape=[
            pltpu.VMEM((rows - skip, groups * run), jnp.bfloat16) for _, run in runs
        ],
        in_specs=[pl.BlockSpec(memory_space=pltpu.VMEM)],
        out_specs=[pl.BlockSpec(memory_space=pltpu.VMEM) for _ in runs],
        cost_estimate=pl.CostEstimate(
            flops=2 * block.size * width, bytes_accessed=4 * block.size, transcendentals=0
        ),
        compiler_params=pltpu.CompilerParams(vmem_limit_bytes=24 << 20),
        name="picks",
    )(block)


def turn_kernel(step, onsets, block, turned, squares):
    rows, width = block.shape
    owner = lax.axis_index("src")
    blocks = lax.axis_size("src")
    top_row = lax.axis_index("tm") * rows
    own_first = onsets[owner] - top_row
    both_first = (
        jnp.maximum(onsets[owner], onsets[lax.rem(owner + blocks - 1, blocks)]) - top_row
    )
    total = jnp.zeros((1, width), jnp.float32)
    for top in range(0, rows, step):
        piece = block[top : top + step, :]
        ids = lax.broadcasted_iota(jnp.int32, (step, width), 0) + top
        wide = jnp.where(ids >= own_first, piece.astype(jnp.float32), 0.0)
        total = total + jnp.sum(wide * wide, axis=0, keepdims=True)
        shown = jnp.where(ids >= both_first, piece.astype(jnp.float32), 0.0)
        turned[:, top : top + step] = shown.T.astype(jnp.bfloat16)
    squares[...] = total


def turn(onsets, block):
    rows, width = block.shape
    step = 128 if rows % 128 == 0 else rows
    return pl.pallas_call(
        functools.partial(turn_kernel, step),
        out_shape=(
            pltpu.VMEM((width, rows), jnp.bfloat16),
            pltpu.VMEM((1, width), jnp.float32),
        ),
        in_specs=[pl.BlockSpec(memory_space=pltpu.SMEM), pl.BlockSpec(memory_space=pltpu.VMEM)],
        out_specs=(pl.BlockSpec(memory_space=pltpu.VMEM),) * 2,
        cost_estimate=pl.CostEstimate(
            flops=4 * block.size, bytes_accessed=4 * block.size, transcendentals=0
        ),
        compiler_params=pltpu.CompilerParams(vmem_limit_bytes=16 << 20),
        name="turn",
    )(onsets, block)


def gram_kernel(share, run, pairs, own, head, rest, keep, give, part):
    cut = head.shape[0]
    columns = rest.shape[1]
    groups = keep.shape[0] * 2
    bit = lax.rem(lax.axis_index("tm"), 2)
    owner_first = pairs[0, 0] == lax.axis_index("src")
    product = jnp.dot(
        own[:, cut:], rest[...], preferred_element_type=jnp.float32
    ) + jnp.dot(
        own[:, :cut], head[...], preferred_element_type=jnp.float32
    )

    @pl.when(owner_first)
    def _():
        part[...] = product
        for pair in range(groups // 2):
            for target, odd in ((keep, bit), (give, 1 - bit)):
                top = (2 * pair + odd) * share
                for piece in range(share // run):
                    rows = pl.ds(pl.multiple_of(top + piece * run, 8), run)
                    target[pair, :, piece * columns : (piece + 1) * columns] = part[rows, :]

    @pl.when(jnp.logical_not(owner_first))
    def _():
        turned = product.T
        for pair in range(groups // 2):
            even = turned[2 * pair * run : (2 * pair + 1) * run, :]
            uneven = turned[(2 * pair + 1) * run : (2 * pair + 2) * run, :]
            keep[pair] = jnp.where(bit == 0, even, uneven)
            give[pair] = jnp.where(bit == 0, uneven, even)


def gram(pairs, own, head, rest, share, run):
    width = own.shape[0]
    groups = width // share
    half = pltpu.VMEM((groups // 2, run, width), jnp.float32)
    columns = groups * run
    return pl.pallas_call(
        functools.partial(gram_kernel, share, run),
        out_shape=(half, half),
        in_specs=[pl.BlockSpec(memory_space=pltpu.SMEM)]
        + [pl.BlockSpec(memory_space=pltpu.VMEM)] * 3,
        out_specs=(pl.BlockSpec(memory_space=pltpu.VMEM),) * 2,
        scratch_shapes=[pltpu.VMEM((width, columns), jnp.float32)],
        cost_estimate=pl.CostEstimate(
            flops=2 * own.size * columns, bytes_accessed=2 * own.size, transcendentals=0
        ),
        compiler_params=pltpu.CompilerParams(vmem_limit_bytes=16 << 20),
        name="gram",
    )(pairs, own, head, rest)


def gram_plain(flags, own, head, rest, share, run):
    width = own.shape[0]
    groups = width // share
    columns = groups * run
    block = jnp.concatenate([head, rest], axis=0)
    product = jnp.dot(own, block, preferred_element_type=jnp.float32)
    strips = jnp.where(
        flags[0] == 1,
        product.reshape(groups, share // run, run, columns)
        .transpose(0, 2, 1, 3)
        .reshape(groups, run, width),
        product.T.reshape(groups, run, width),
    )
    return split(strips, flags[1])


def put_back(runs, share, parts):
    width = parts[0].shape[1]
    total = jnp.zeros((share, width), jnp.float32)
    for (start, run), part in zip(runs, parts):
        columns = width // share * run
        spread = (
            part.reshape(run, share // run, columns).transpose(1, 0, 2).reshape(share, columns)
        )
        total = total + lax.dot_general(
            spread,
            picker(width, share, start, run).astype(jnp.float32),
            (((1,), (1,)), ((), ())),
            precision=lax.Precision.HIGHEST,
            preferred_element_type=jnp.float32,
        )
    return total


def fold_kernel(keep, arrived, mine, *gives):
    me = lax.axis_index("tm") // 2
    mine[...] = keep[me] + arrived[me]
    for m, give in enumerate(gives, 1):
        give[...] = keep[me ^ m] + arrived[me ^ m]


def fold(keep, arrived):
    strip = pltpu.VMEM(keep.shape[1:], jnp.float32)
    return pl.pallas_call(
        fold_kernel,
        out_shape=[strip] * keep.shape[0],
        in_specs=[pl.BlockSpec(memory_space=pltpu.VMEM)] * 2,
        out_specs=[pl.BlockSpec(memory_space=pltpu.VMEM)] * keep.shape[0],
        cost_estimate=pl.CostEstimate(
            flops=keep.size, bytes_accessed=12 * keep.size, transcendentals=0
        ),
        compiler_params=pltpu.CompilerParams(vmem_limit_bytes=8 << 20),
        name="fold",
    )(keep, arrived)


def plus_kernel(a, b, out):
    out[...] = a[...] + b[...]


def plus(a, b):
    return pl.pallas_call(
        plus_kernel,
        out_shape=pltpu.VMEM(a.shape, a.dtype),
        in_specs=[pl.BlockSpec(memory_space=pltpu.VMEM)] * 2,
        out_specs=pl.BlockSpec(memory_space=pltpu.VMEM),
        compiler_params=pltpu.CompilerParams(vmem_limit_bytes=1 << 20),
        name="plus",
    )(a, b)


def placed(owner_first, share, start, run, terms, total):
    width = total.shape[1]
    columns = width // share * run
    part = terms[0][...]
    for term in terms[1:]:
        part = part + term[...]

    @pl.when(owner_first)
    def _():
        spread = jnp.concatenate(
            [part[:, n * columns : (n + 1) * columns] for n in range(share // run)], axis=0
        )
        q = lax.broadcasted_iota(jnp.int32, (columns, width), 0)
        source = lax.broadcasted_iota(jnp.int32, (columns, width), 1)
        order = (q // run) * share + start + q % run == source
        total[...] += jnp.dot(
            spread,
            order.astype(jnp.float32),
            precision=lax.Precision.HIGHEST,
            preferred_element_type=jnp.float32,
        )

    @pl.when(jnp.logical_not(owner_first))
    def _():
        total[start : start + run, :] = part


def place_kernel(share, start, run, pairs, *refs):
    *terms, total = refs
    if len(terms) > 4:
        total[...] = terms.pop()[...]
    else:
        total[...] = jnp.zeros_like(total)
    placed(pairs[0, 0] == lax.axis_index("src"), share, start, run, terms, total)


def finish_kernel(share, start, run, pairs, base, norm_own, norm_low, *refs):
    *terms, out, total = refs
    width = total.shape[1]
    owner_first = pairs[0, 0] == lax.axis_index("src")
    total[...] = base[...]
    placed(owner_first, share, start, run, terms, total)
    scale_own = lax.rsqrt(norm_own[...] + 1e-06)
    scale_low = lax.rsqrt(norm_low[...] + 1e-06)
    scale_first = jnp.where(owner_first, scale_own, scale_low)
    scale_second = jnp.where(owner_first, scale_low, scale_own)
    row = lax.broadcasted_iota(jnp.int32, (share, width), 0) + lax.axis_index("tm") * share
    column = lax.broadcasted_iota(jnp.int32, (share, width), 1)
    scale_rows = jnp.sum(jnp.where(row == column, scale_first, 0.0), axis=1, keepdims=True)
    out[0] = total[...] * scale_rows * scale_second


def place(pairs, terms, base, share, width, start, run):
    given = list(terms) + ([] if base is None else [base])
    return pl.pallas_call(
        functools.partial(place_kernel, share, start, run),
        out_shape=pltpu.VMEM((share, width), jnp.float32),
        in_specs=[pl.BlockSpec(memory_space=pltpu.SMEM)]
        + [pl.BlockSpec(memory_space=pltpu.VMEM)] * len(given),
        out_specs=pl.BlockSpec(memory_space=pltpu.VMEM),
        cost_estimate=pl.CostEstimate(
            flops=2 * share * width * 256, bytes_accessed=8 * share * width, transcendentals=0
        ),
        compiler_params=pltpu.CompilerParams(vmem_limit_bytes=8 << 20),
        name="place",
    )(pairs, *given)


def finish(pairs, base, norm_own, norm_low, terms, share, start, run):
    return pl.pallas_call(
        functools.partial(finish_kernel, share, start, run),
        out_shape=jax.ShapeDtypeStruct((1,) + base.shape, jnp.float32),
        in_specs=[pl.BlockSpec(memory_space=pltpu.SMEM)]
        + [pl.BlockSpec(memory_space=pltpu.VMEM)] * (3 + len(terms)),
        out_specs=pl.BlockSpec(memory_space=pltpu.VMEM),
        scratch_shapes=[pltpu.VMEM(base.shape, jnp.float32)],
        cost_estimate=pl.CostEstimate(
            flops=2 * base.size * 256, bytes_accessed=8 * base.size, transcendentals=0
        ),
        compiler_params=pltpu.CompilerParams(vmem_limit_bytes=8 << 20),
        name="finish",
    )(pairs, base, norm_own, norm_low, *terms)


def on_device(greens, pairs, onsets):
    rows_dev, width = greens.shape
    groups = lax.axis_size("tm")
    share = width // groups
    runs = runs_of(share)
    aligned = groups == 8 and all(run % 8 == 0 and groups * run % 128 == 0 for _, run in runs)
    cut = rows_dev // HEAD

    head = from_behind(greens[:cut], "src", 1)
    chosen = picks(greens, share, runs, cut)
    lower = []
    for block in chosen:
        lower.append(from_behind(block, "src", 1))
    own, squares = turn(onsets, greens)
    norm_own = summed(squares, "tm")
    norm_low = from_behind(norm_own, "src", 1)
    heads = picks(head, share, runs, 0)
    if not aligned:
        return plain_tail(pairs, own, heads, lower, norm_own[0], norm_low[0], share, runs)

    base = None
    for step, (run, top, block) in enumerate(zip(runs, heads, lower)):
        keep, give = gram(pairs, own, top, block, share, run[1])
        arrived = swapped(give, "tm", 1)
        mine, *gives = fold(keep, arrived)
        terms = [mine]
        for m, strip in enumerate(gives, 1):
            terms.append(swapped(strip, "tm", 2 * m))
        if step < len(runs) - 1:
            base = place(pairs, terms, base, share, width, *run)
    return finish(pairs, base, norm_own, norm_low, terms, share, *runs[-1])


def plain_tail(pairs, own, heads, lower, norm_own, norm_low, share, runs):
    row_group = lax.axis_index("tm")
    owner_first = pairs[0, 0] == lax.axis_index("src")
    flags = jnp.stack([owner_first.astype(jnp.int32), row_group % 2])
    parts = []
    for run, top, block in zip(runs, heads, lower):
        keep, give = gram_plain(flags, own, top, block, share, run[1])
        parts.append(functools.reduce(jnp.add, strips_arrived(keep, give, "tm")))
    scale_own = lax.rsqrt(norm_own + 1e-06)
    scale_low = lax.rsqrt(norm_low + 1e-06)
    scale_rows = lax.dynamic_slice_in_dim(
        jnp.where(owner_first, scale_own, scale_low), row_group * share, share, 0
    )[:, None]
    scale_cols = jnp.where(owner_first, scale_low, scale_own)[None, :]
    base = jnp.where(
        owner_first, put_back(runs, share, parts), jnp.concatenate(parts, axis=0)
    )
    return (base * scale_rows * scale_cols)[None]


def solution(mesh):
    in_specs = (P("tm", "src"), P("src", None), P())
    out_specs = P("src", "tm", None)
    return jax.shard_map(
        on_device, mesh=mesh, in_specs=in_specs, out_specs=out_specs, check_vma=False
    )
```

```python
import functools

import jax
import jax.numpy as jnp
from jax import lax
from jax.experimental import pallas as pl
from jax.experimental.pallas import tpu as pltpu
from jax.sharding import PartitionSpec as P


PARTS = (2, 2, 1, 1)
HEAD = 8


def from_behind(value, axis, by):
    length = lax.axis_size(axis)
    return lax.ppermute(value, axis, [(i, (i + by) % length) for i in range(length)])


def swapped(value, axis, bits):
    length = lax.axis_size(axis)
    return lax.ppermute(value, axis, [(i, i ^ bits) for i in range(length)])


def summed(value, axis):
    bits = 1
    while bits < lax.axis_size(axis):
        value = plus(value, swapped(value, axis, bits))
        bits *= 2
    return value


def split(strips, bit):
    halves = strips.reshape((strips.shape[0] // 2, 2) + strips.shape[1:])
    keep = lax.dynamic_index_in_dim(halves, bit, 1, keepdims=False)
    give = lax.dynamic_index_in_dim(halves, 1 - bit, 1, keepdims=False)
    return keep, give


def strips_arrived(keep, give, axis):
    me = lax.axis_index(axis) // 2
    bits = 1
    strips = keep + swapped(give, axis, bits)
    while strips.shape[0] > 4:
        keep, give = split(strips, me % 2)
        bits *= 2
        me = me // 2
        strips = keep + swapped(give, axis, bits)
    bits *= 2
    terms = [lax.dynamic_index_in_dim(strips, me, 0, keepdims=False)]
    for m in range(1, strips.shape[0]):
        give = lax.dynamic_index_in_dim(strips, me ^ m, 0, keepdims=False)
        terms.append(swapped(give, axis, bits * m))
    return terms


def runs_of(share):
    whole = sum(PARTS)
    if share % whole:
        return [(0, share)]
    unit = share // whole
    runs, start = [], 0
    for part in PARTS:
        runs.append((start, part * unit))
        start += part * unit
    return runs


def picker(width, share, start, run):
    picked = width // share * run
    q = lax.broadcasted_iota(jnp.int32, (width, picked), 1)
    source = lax.broadcasted_iota(jnp.int32, (width, picked), 0)
    return (q // run) * share + start + q % run == source


def picks_kernel(share, runs, skip, block, *outs):
    width = block.shape[1]
    source = block[skip:, :]
    for (start, run), out in zip(runs, outs):
        order = picker(width, share, start, run).astype(jnp.float32).astype(jnp.bfloat16)
        out[...] = jnp.dot(source, order, preferred_element_type=jnp.float32).astype(jnp.bfloat16)


def picks(block, share, runs, skip):
    rows, width = block.shape
    groups = width // share
    return pl.pallas_call(
        functools.partial(picks_kernel, share, runs, skip),
        out_shape=[
            pltpu.VMEM((rows - skip, groups * run), jnp.bfloat16) for _, run in runs
        ],
        in_specs=[pl.BlockSpec(memory_space=pltpu.VMEM)],
        out_specs=[pl.BlockSpec(memory_space=pltpu.VMEM) for _ in runs],
        cost_estimate=pl.CostEstimate(
            flops=2 * block.size * width, bytes_accessed=4 * block.size, transcendentals=0
        ),
        compiler_params=pltpu.CompilerParams(vmem_limit_bytes=24 << 20),
        name="picks",
    )(block)


def turn_kernel(step, onsets, block, turned, squares):
    rows, width = block.shape
    owner = lax.axis_index("src")
    blocks = lax.axis_size("src")
    top_row = lax.axis_index("tm") * rows
    own_first = onsets[owner] - top_row
    both_first = (
        jnp.maximum(onsets[owner], onsets[lax.rem(owner + blocks - 1, blocks)]) - top_row
    )
    total = jnp.zeros((1, width), jnp.float32)
    for top in range(0, rows, step):
        piece = block[top : top + step, :]
        ids = lax.broadcasted_iota(jnp.int32, (step, width), 0) + top
        wide = jnp.where(ids >= own_first, piece.astype(jnp.float32), 0.0)
        total = total + jnp.sum(wide * wide, axis=0, keepdims=True)
        shown = jnp.where(ids >= both_first, piece.astype(jnp.float32), 0.0)
        turned[:, top : top + step] = shown.T.astype(jnp.bfloat16)
    squares[...] = total


def turn(onsets, block):
    rows, width = block.shape
    step = 128 if rows % 128 == 0 else rows
    return pl.pallas_call(
        functools.partial(turn_kernel, step),
        out_shape=(
            pltpu.VMEM((width, rows), jnp.bfloat16),
            pltpu.VMEM((1, width), jnp.float32),
        ),
        in_specs=[pl.BlockSpec(memory_space=pltpu.SMEM), pl.BlockSpec(memory_space=pltpu.VMEM)],
        out_specs=(pl.BlockSpec(memory_space=pltpu.VMEM),) * 2,
        cost_estimate=pl.CostEstimate(
            flops=4 * block.size, bytes_accessed=4 * block.size, transcendentals=0
        ),
        compiler_params=pltpu.CompilerParams(vmem_limit_bytes=16 << 20),
        name="turn",
    )(onsets, block)


def gram_kernel(share, run, pairs, own, head, rest, keep, give, part):
    cut = head.shape[0]
    columns = rest.shape[1]
    groups = keep.shape[0] * 2
    bit = lax.rem(lax.axis_index("tm"), 2)
    owner_first = pairs[0, 0] == lax.axis_index("src")
    product = jnp.dot(
        own[:, cut:], rest[...], preferred_element_type=jnp.float32
    ) + jnp.dot(
        own[:, :cut], head[...], preferred_element_type=jnp.float32
    )

    @pl.when(owner_first)
    def _():
        part[...] = product
        for pair in range(groups // 2):
            for target, odd in ((keep, bit), (give, 1 - bit)):
                top = (2 * pair + odd) * share
                for piece in range(share // run):
                    rows = pl.ds(pl.multiple_of(top + piece * run, 8), run)
                    target[pair, :, piece * columns : (piece + 1) * columns] = part[rows, :]

    @pl.when(jnp.logical_not(owner_first))
    def _():
        turned = product.T
        for pair in range(groups // 2):
            even = turned[2 * pair * run : (2 * pair + 1) * run, :]
            uneven = turned[(2 * pair + 1) * run : (2 * pair + 2) * run, :]
            keep[pair] = jnp.where(bit == 0, even, uneven)
            give[pair] = jnp.where(bit == 0, uneven, even)


def gram(pairs, own, head, rest, share, run):
    width = own.shape[0]
    groups = width // share
    half = pltpu.VMEM((groups // 2, run, width), jnp.float32)
    columns = groups * run
    return pl.pallas_call(
        functools.partial(gram_kernel, share, run),
        out_shape=(half, half),
        in_specs=[pl.BlockSpec(memory_space=pltpu.SMEM)]
        + [pl.BlockSpec(memory_space=pltpu.VMEM)] * 3,
        out_specs=(pl.BlockSpec(memory_space=pltpu.VMEM),) * 2,
        scratch_shapes=[pltpu.VMEM((width, columns), jnp.float32)],
        cost_estimate=pl.CostEstimate(
            flops=2 * own.size * columns, bytes_accessed=2 * own.size, transcendentals=0
        ),
        compiler_params=pltpu.CompilerParams(vmem_limit_bytes=16 << 20),
        name="gram",
    )(pairs, own, head, rest)


def gram_plain(flags, own, head, rest, share, run):
    width = own.shape[0]
    groups = width // share
    columns = groups * run
    block = jnp.concatenate([head, rest], axis=0)
    product = jnp.dot(own, block, preferred_element_type=jnp.float32)
    strips = jnp.where(
        flags[0] == 1,
        product.reshape(groups, share // run, run, columns)
        .transpose(0, 2, 1, 3)
        .reshape(groups, run, width),
        product.T.reshape(groups, run, width),
    )
    return split(strips, flags[1])


def put_back(runs, share, parts):
    width = parts[0].shape[1]
    total = jnp.zeros((share, width), jnp.float32)
    for (start, run), part in zip(runs, parts):
        columns = width // share * run
        spread = (
            part.reshape(run, share // run, columns).transpose(1, 0, 2).reshape(share, columns)
        )
        total = total + lax.dot_general(
            spread,
            picker(width, share, start, run).astype(jnp.float32),
            (((1,), (1,)), ((), ())),
            precision=lax.Precision.HIGHEST,
            preferred_element_type=jnp.float32,
        )
    return total


def fold_kernel(keep, arrived, mine, *gives):
    me = lax.axis_index("tm") // 2
    mine[...] = keep[me] + arrived[me]
    for m, give in enumerate(gives, 1):
        give[...] = keep[me ^ m] + arrived[me ^ m]


def fold(keep, arrived):
    strip = pltpu.VMEM(keep.shape[1:], jnp.float32)
    return pl.pallas_call(
        fold_kernel,
        out_shape=[strip] * keep.shape[0],
        in_specs=[pl.BlockSpec(memory_space=pltpu.VMEM)] * 2,
        out_specs=[pl.BlockSpec(memory_space=pltpu.VMEM)] * keep.shape[0],
        cost_estimate=pl.CostEstimate(
            flops=keep.size, bytes_accessed=12 * keep.size, transcendentals=0
        ),
        compiler_params=pltpu.CompilerParams(vmem_limit_bytes=8 << 20),
        name="fold",
    )(keep, arrived)


def plus_kernel(a, b, out):
    out[...] = a[...] + b[...]


def plus(a, b):
    return pl.pallas_call(
        plus_kernel,
        out_shape=pltpu.VMEM(a.shape, a.dtype),
        in_specs=[pl.BlockSpec(memory_space=pltpu.VMEM)] * 2,
        out_specs=pl.BlockSpec(memory_space=pltpu.VMEM),
        compiler_params=pltpu.CompilerParams(vmem_limit_bytes=1 << 20),
        name="plus",
    )(a, b)


def placed(owner_first, share, start, run, terms, total, scales=None):
    width = total.shape[1]
    columns = width // share * run
    part = terms[0][...]
    for term in terms[1:]:
        part = part + term[...]

    @pl.when(owner_first)
    def _():
        spread = jnp.concatenate(
            [part[:, n * columns : (n + 1) * columns] for n in range(share // run)], axis=0
        )
        left = spread * 0.0625
        pieces = []
        for _ in range(3):
            pieces.append(left.astype(jnp.bfloat16))
            left = left - pieces[-1].astype(jnp.float32)
        q = lax.broadcasted_iota(jnp.int32, (columns, width), 0)
        source = lax.broadcasted_iota(jnp.int32, (columns, width), 1)
        order = (q // run) * share + start + q % run == source
        spots = jnp.dot(
            jnp.concatenate(pieces, axis=0),
            order.astype(jnp.float32).astype(jnp.bfloat16),
            preferred_element_type=jnp.float32,
        )
        added = (spots[:share] + spots[share : 2 * share] + spots[2 * share :]) * 16.0
        if scales is not None:
            added = added * scales[0][:, :1] * scales[1][...]
        total[...] += added

    @pl.when(jnp.logical_not(owner_first))
    def _():
        rows = part
        if scales is not None:
            rows = rows * scales[0][start : start + run, :1] * scales[1][...]
        total[start : start + run, :] = rows


def place_kernel(share, start, run, pairs, *refs):
    *terms, total = refs
    if len(terms) > 4:
        total[...] = terms.pop()[...]
    else:
        total[...] = jnp.zeros_like(total)
    placed(pairs[0, 0] == lax.axis_index("src"), share, start, run, terms, total)


def scales_kernel(share, pairs, norm_own, norm_low, rows, columns):
    width = columns.shape[1]
    owner_first = pairs[0, 0] == lax.axis_index("src")
    scale_own = lax.rsqrt(norm_own[...] + 1e-06)
    scale_low = lax.rsqrt(norm_low[...] + 1e-06)
    scale_first = jnp.where(owner_first, scale_own, scale_low)
    row = lax.broadcasted_iota(jnp.int32, (share, width), 0) + lax.axis_index("tm") * share
    column = lax.broadcasted_iota(jnp.int32, (share, width), 1)
    mine = jnp.sum(jnp.where(row == column, scale_first, 0.0), axis=1, keepdims=True)
    rows[...] = jnp.broadcast_to(mine, rows.shape)
    columns[...] = jnp.where(owner_first, scale_low, scale_own)


def finish_kernel(share, start, run, pairs, base, rows, columns, *refs):
    *terms, out = refs
    owner_first = pairs[0, 0] == lax.axis_index("src")
    out[0] = base[...] * rows[:, :1] * columns[...]
    placed(owner_first, share, start, run, terms, out.at[0], (rows, columns))


def small_call(kernel, out_shape, pairs, given, flops):
    return pl.pallas_call(
        kernel,
        out_shape=out_shape,
        in_specs=[pl.BlockSpec(memory_space=pltpu.SMEM)]
        + [pl.BlockSpec(memory_space=pltpu.VMEM)] * len(given),
        out_specs=jax.tree.map(lambda _: pl.BlockSpec(memory_space=pltpu.VMEM), out_shape),
        cost_estimate=pl.CostEstimate(
            flops=flops,
            bytes_accessed=sum(4 * x.size for x in given),
            transcendentals=0,
        ),
        compiler_params=pltpu.CompilerParams(vmem_limit_bytes=8 << 20),
    )(pairs, *given)


def place(pairs, terms, base, share, width, start, run):
    return small_call(
        functools.partial(place_kernel, share, start, run),
        pltpu.VMEM((share, width), jnp.float32),
        pairs,
        list(terms) + ([] if base is None else [base]),
        2 * share * width * 256,
    )


def scales_of(pairs, norm_own, norm_low, share):
    width = norm_own.shape[1]
    return small_call(
        functools.partial(scales_kernel, share),
        (pltpu.VMEM((share, 128), jnp.float32), pltpu.VMEM((1, width), jnp.float32)),
        pairs,
        [norm_own, norm_low],
        share * width,
    )


def finish(pairs, base, scales, terms, share, start, run):
    return small_call(
        functools.partial(finish_kernel, share, start, run),
        jax.ShapeDtypeStruct((1,) + base.shape, jnp.float32),
        pairs,
        [base, *scales, *terms],
        2 * base.size * 256,
    )


def top_kernel(block, out):
    pltpu.sync_copy(block.at[pl.ds(0, out.shape[0])], out)


def top_of(block, rows):
    return pl.pallas_call(
        top_kernel,
        out_shape=pltpu.VMEM((rows,) + block.shape[1:], block.dtype),
        in_specs=[pl.BlockSpec(memory_space=pltpu.HBM)],
        out_specs=pl.BlockSpec(memory_space=pltpu.VMEM),
        compiler_params=pltpu.CompilerParams(vmem_limit_bytes=60 << 20),
        name="top",
    )(block)


def on_device(greens, pairs, onsets):
    rows_dev, width = greens.shape
    groups = lax.axis_size("tm")
    share = width // groups
    runs = runs_of(share)
    aligned = groups == 8 and all(run % 8 == 0 and groups * run % 128 == 0 for _, run in runs)
    cut = rows_dev // HEAD

    head = from_behind(top_of(greens, cut), "src", 1)
    chosen = picks(greens, share, runs, cut)
    lower = []
    for block in chosen:
        lower.append(from_behind(block, "src", 1))
    own, squares = turn(onsets, greens)
    norm_own = summed(squares, "tm")
    norm_low = from_behind(norm_own, "src", 1)
    heads = picks(head, share, runs, 0)
    if not aligned:
        return plain_tail(pairs, own, heads, lower, norm_own[0], norm_low[0], share, runs)

    base = None
    for step, (run, top, block) in enumerate(zip(runs, heads, lower)):
        keep, give = gram(pairs, own, top, block, share, run[1])
        arrived = swapped(give, "tm", 1)
        mine, *gives = fold(keep, arrived)
        terms = [mine]
        for m, strip in enumerate(gives, 1):
            terms.append(swapped(strip, "tm", 2 * m))
        if step < len(runs) - 1:
            base = place(pairs, terms, base, share, width, *run)
    scales = scales_of(pairs, norm_own, norm_low, share)
    return finish(pairs, base, scales, terms, share, *runs[-1])


def plain_tail(pairs, own, heads, lower, norm_own, norm_low, share, runs):
    row_group = lax.axis_index("tm")
    owner_first = pairs[0, 0] == lax.axis_index("src")
    flags = jnp.stack([owner_first.astype(jnp.int32), row_group % 2])
    parts = []
    for run, top, block in zip(runs, heads, lower):
        keep, give = gram_plain(flags, own, top, block, share, run[1])
        parts.append(functools.reduce(jnp.add, strips_arrived(keep, give, "tm")))
    scale_own = lax.rsqrt(norm_own + 1e-06)
    scale_low = lax.rsqrt(norm_low + 1e-06)
    scale_rows = lax.dynamic_slice_in_dim(
        jnp.where(owner_first, scale_own, scale_low), row_group * share, share, 0
    )[:, None]
    scale_cols = jnp.where(owner_first, scale_low, scale_own)[None, :]
    base = jnp.where(
        owner_first, put_back(runs, share, parts), jnp.concatenate(parts, axis=0)
    )
    return (base * scale_rows * scale_cols)[None]


def solution(mesh):
    in_specs = (P("tm", "src"), P("src", None), P())
    out_specs = P("src", "tm", None)
    return jax.shard_map(
        on_device, mesh=mesh, in_specs=in_specs, out_specs=out_specs, check_vma=False
    )
```

```python
import functools

import jax
import jax.numpy as jnp
from jax import lax
from jax.experimental import pallas as pl
from jax.experimental.pallas import tpu as pltpu
from jax.sharding import PartitionSpec as P


PARTS = (2, 2, 1, 1)
HEAD = 8
LATE = 4


def from_behind(value, axis, by):
    length = lax.axis_size(axis)
    return lax.ppermute(value, axis, [(i, (i + by) % length) for i in range(length)])


def swapped(value, axis, bits):
    length = lax.axis_size(axis)
    return lax.ppermute(value, axis, [(i, i ^ bits) for i in range(length)])


def summed(value, axis):
    bits = 1
    while bits < lax.axis_size(axis):
        value = plus(value, swapped(value, axis, bits))
        bits *= 2
    return value


def split(strips, bit):
    halves = strips.reshape((strips.shape[0] // 2, 2) + strips.shape[1:])
    keep = lax.dynamic_index_in_dim(halves, bit, 1, keepdims=False)
    give = lax.dynamic_index_in_dim(halves, 1 - bit, 1, keepdims=False)
    return keep, give


def strips_arrived(keep, give, axis):
    me = lax.axis_index(axis) // 2
    bits = 1
    strips = keep + swapped(give, axis, bits)
    while strips.shape[0] > 4:
        keep, give = split(strips, me % 2)
        bits *= 2
        me = me // 2
        strips = keep + swapped(give, axis, bits)
    bits *= 2
    terms = [lax.dynamic_index_in_dim(strips, me, 0, keepdims=False)]
    for m in range(1, strips.shape[0]):
        give = lax.dynamic_index_in_dim(strips, me ^ m, 0, keepdims=False)
        terms.append(swapped(give, axis, bits * m))
    return terms


def runs_of(share):
    whole = sum(PARTS)
    if share % whole:
        return [(0, share)]
    unit = share // whole
    runs, start = [], 0
    for part in PARTS:
        runs.append((start, part * unit))
        start += part * unit
    return runs


def picker(width, share, start, run):
    picked = width // share * run
    q = lax.broadcasted_iota(jnp.int32, (width, picked), 1)
    source = lax.broadcasted_iota(jnp.int32, (width, picked), 0)
    return (q // run) * share + start + q % run == source


def picks_kernel(share, pieces, block, *outs):
    width = block.shape[1]
    for (low, high, start, run), out in zip(pieces, outs):
        order = picker(width, share, start, run).astype(jnp.float32).astype(jnp.bfloat16)
        out[...] = jnp.dot(
            block[low:high, :], order, preferred_element_type=jnp.float32
        ).astype(jnp.bfloat16)


def picks(block, share, pieces):
    width = block.shape[1]
    groups = width // share
    return pl.pallas_call(
        functools.partial(picks_kernel, share, pieces),
        out_shape=[
            pltpu.VMEM((high - low, groups * run), jnp.bfloat16) for low, high, _, run in pieces
        ],
        in_specs=[pl.BlockSpec(memory_space=pltpu.VMEM)],
        out_specs=[pl.BlockSpec(memory_space=pltpu.VMEM) for _ in pieces],
        cost_estimate=pl.CostEstimate(
            flops=2 * block.size * width, bytes_accessed=4 * block.size, transcendentals=0
        ),
        compiler_params=pltpu.CompilerParams(vmem_limit_bytes=24 << 20),
        name="picks",
    )(block)


def turn_kernel(step, onsets, block, turned, squares):
    rows, width = block.shape
    owner = lax.axis_index("src")
    blocks = lax.axis_size("src")
    top_row = lax.axis_index("tm") * rows
    own_first = onsets[owner] - top_row
    both_first = (
        jnp.maximum(onsets[owner], onsets[lax.rem(owner + blocks - 1, blocks)]) - top_row
    )
    total = jnp.zeros((1, width), jnp.float32)
    for top in range(0, rows, step):
        piece = block[top : top + step, :]
        ids = lax.broadcasted_iota(jnp.int32, (step, width), 0) + top
        wide = jnp.where(ids >= own_first, piece.astype(jnp.float32), 0.0)
        total = total + jnp.sum(wide * wide, axis=0, keepdims=True)
        shown = jnp.where(ids >= both_first, piece.astype(jnp.float32), 0.0)
        turned[:, top : top + step] = shown.T.astype(jnp.bfloat16)
    squares[...] = total


def turn(onsets, block):
    rows, width = block.shape
    step = 128 if rows % 128 == 0 else rows
    return pl.pallas_call(
        functools.partial(turn_kernel, step),
        out_shape=(
            pltpu.VMEM((width, rows), jnp.bfloat16),
            pltpu.VMEM((1, width), jnp.float32),
        ),
        in_specs=[pl.BlockSpec(memory_space=pltpu.SMEM), pl.BlockSpec(memory_space=pltpu.VMEM)],
        out_specs=(pl.BlockSpec(memory_space=pltpu.VMEM),) * 2,
        cost_estimate=pl.CostEstimate(
            flops=4 * block.size, bytes_accessed=4 * block.size, transcendentals=0
        ),
        compiler_params=pltpu.CompilerParams(vmem_limit_bytes=16 << 20),
        name="turn",
    )(onsets, block)


def product_of(own, ranges, refs):
    return functools.reduce(
        jnp.add,
        (
            jnp.dot(own[:, low:high], ref[...], preferred_element_type=jnp.float32)
            for (low, high), ref in zip(ranges, refs)
        ),
    )


def early_kernel(ranges, own, *refs):
    *rows, out = refs
    out[...] = product_of(own, ranges, rows)


def early(own, ranges, blocks):
    columns = blocks[0].shape[1]
    return pl.pallas_call(
        functools.partial(early_kernel, ranges),
        out_shape=pltpu.VMEM((own.shape[0], columns), jnp.float32),
        in_specs=[pl.BlockSpec(memory_space=pltpu.VMEM)] * (1 + len(blocks)),
        out_specs=pl.BlockSpec(memory_space=pltpu.VMEM),
        cost_estimate=pl.CostEstimate(
            flops=2 * own.size * columns, bytes_accessed=2 * own.size, transcendentals=0
        ),
        compiler_params=pltpu.CompilerParams(vmem_limit_bytes=16 << 20),
        name="early",
    )(own, *blocks)


def gram_kernel(share, run, ranges, pairs, own, *refs):
    *rows, keep, give, part = refs
    columns = rows[0].shape[1]
    groups = keep.shape[0] * 2
    bit = lax.rem(lax.axis_index("tm"), 2)
    owner_first = pairs[0, 0] == lax.axis_index("src")
    product = product_of(own, ranges, rows)
    if len(rows) > len(ranges):
        product = product + rows[-1][...]

    @pl.when(owner_first)
    def _():
        part[...] = product
        for pair in range(groups // 2):
            for target, odd in ((keep, bit), (give, 1 - bit)):
                top = (2 * pair + odd) * share
                for piece in range(share // run):
                    rows = pl.ds(pl.multiple_of(top + piece * run, 8), run)
                    target[pair, :, piece * columns : (piece + 1) * columns] = part[rows, :]

    @pl.when(jnp.logical_not(owner_first))
    def _():
        turned = product.T
        for pair in range(groups // 2):
            even = turned[2 * pair * run : (2 * pair + 1) * run, :]
            uneven = turned[(2 * pair + 1) * run : (2 * pair + 2) * run, :]
            keep[pair] = jnp.where(bit == 0, even, uneven)
            give[pair] = jnp.where(bit == 0, uneven, even)


def gram(pairs, own, ranges, blocks, share, run):
    width = own.shape[0]
    groups = width // share
    half = pltpu.VMEM((groups // 2, run, width), jnp.float32)
    columns = groups * run
    return pl.pallas_call(
        functools.partial(gram_kernel, share, run, ranges),
        out_shape=(half, half),
        in_specs=[pl.BlockSpec(memory_space=pltpu.SMEM)]
        + [pl.BlockSpec(memory_space=pltpu.VMEM)] * (1 + len(blocks)),
        out_specs=(pl.BlockSpec(memory_space=pltpu.VMEM),) * 2,
        scratch_shapes=[pltpu.VMEM((width, columns), jnp.float32)],
        cost_estimate=pl.CostEstimate(
            flops=2 * own.size * columns, bytes_accessed=2 * own.size, transcendentals=0
        ),
        compiler_params=pltpu.CompilerParams(vmem_limit_bytes=16 << 20),
        name="gram",
    )(pairs, own, *blocks)


def gram_plain(flags, own, blocks, share, run):
    width = own.shape[0]
    groups = width // share
    columns = groups * run
    block = jnp.concatenate(blocks, axis=0)
    product = jnp.dot(own, block, preferred_element_type=jnp.float32)
    strips = jnp.where(
        flags[0] == 1,
        product.reshape(groups, share // run, run, columns)
        .transpose(0, 2, 1, 3)
        .reshape(groups, run, width),
        product.T.reshape(groups, run, width),
    )
    return split(strips, flags[1])


def put_back(runs, share, parts):
    width = parts[0].shape[1]
    total = jnp.zeros((share, width), jnp.float32)
    for (start, run), part in zip(runs, parts):
        columns = width // share * run
        spread = (
            part.reshape(run, share // run, columns).transpose(1, 0, 2).reshape(share, columns)
        )
        total = total + lax.dot_general(
            spread,
            picker(width, share, start, run).astype(jnp.float32),
            (((1,), (1,)), ((), ())),
            precision=lax.Precision.HIGHEST,
            preferred_element_type=jnp.float32,
        )
    return total


def fold_kernel(keep, arrived, mine, *gives):
    me = lax.axis_index("tm") // 2
    mine[...] = keep[me] + arrived[me]
    for m, give in enumerate(gives, 1):
        give[...] = keep[me ^ m] + arrived[me ^ m]


def fold(keep, arrived):
    strip = pltpu.VMEM(keep.shape[1:], jnp.float32)
    return pl.pallas_call(
        fold_kernel,
        out_shape=[strip] * keep.shape[0],
        in_specs=[pl.BlockSpec(memory_space=pltpu.VMEM)] * 2,
        out_specs=[pl.BlockSpec(memory_space=pltpu.VMEM)] * keep.shape[0],
        cost_estimate=pl.CostEstimate(
            flops=keep.size, bytes_accessed=12 * keep.size, transcendentals=0
        ),
        compiler_params=pltpu.CompilerParams(vmem_limit_bytes=8 << 20),
        name="fold",
    )(keep, arrived)


def plus_kernel(a, b, out):
    out[...] = a[...] + b[...]


def plus(a, b):
    return pl.pallas_call(
        plus_kernel,
        out_shape=pltpu.VMEM(a.shape, a.dtype),
        in_specs=[pl.BlockSpec(memory_space=pltpu.VMEM)] * 2,
        out_specs=pl.BlockSpec(memory_space=pltpu.VMEM),
        compiler_params=pltpu.CompilerParams(vmem_limit_bytes=1 << 20),
        name="plus",
    )(a, b)


def placed(owner_first, share, start, run, terms, total, scales=None):
    width = total.shape[1]
    columns = width // share * run
    part = terms[0][...]
    for term in terms[1:]:
        part = part + term[...]

    @pl.when(owner_first)
    def _():
        spread = jnp.concatenate(
            [part[:, n * columns : (n + 1) * columns] for n in range(share // run)], axis=0
        )
        left = spread * 0.0625
        pieces = []
        for _ in range(3):
            pieces.append(left.astype(jnp.bfloat16))
            left = left - pieces[-1].astype(jnp.float32)
        q = lax.broadcasted_iota(jnp.int32, (columns, width), 0)
        source = lax.broadcasted_iota(jnp.int32, (columns, width), 1)
        order = (q // run) * share + start + q % run == source
        spots = jnp.dot(
            jnp.concatenate(pieces, axis=0),
            order.astype(jnp.float32).astype(jnp.bfloat16),
            preferred_element_type=jnp.float32,
        )
        added = (spots[:share] + spots[share : 2 * share] + spots[2 * share :]) * 16.0
        if scales is not None:
            added = added * scales[0][:, :1] * scales[1][...]
        total[...] += added

    @pl.when(jnp.logical_not(owner_first))
    def _():
        rows = part
        if scales is not None:
            rows = rows * scales[0][start : start + run, :1] * scales[1][...]
        total[start : start + run, :] = rows


def place_kernel(share, start, run, pairs, *refs):
    *terms, total = refs
    if len(terms) > 4:
        total[...] = terms.pop()[...]
    else:
        total[...] = jnp.zeros_like(total)
    placed(pairs[0, 0] == lax.axis_index("src"), share, start, run, terms, total)


def scales_kernel(share, pairs, norm_own, norm_low, rows, columns):
    width = columns.shape[1]
    owner_first = pairs[0, 0] == lax.axis_index("src")
    scale_own = lax.rsqrt(norm_own[...] + 1e-06)
    scale_low = lax.rsqrt(norm_low[...] + 1e-06)
    scale_first = jnp.where(owner_first, scale_own, scale_low)
    row = lax.broadcasted_iota(jnp.int32, (share, width), 0) + lax.axis_index("tm") * share
    column = lax.broadcasted_iota(jnp.int32, (share, width), 1)
    mine = jnp.sum(jnp.where(row == column, scale_first, 0.0), axis=1, keepdims=True)
    rows[...] = jnp.broadcast_to(mine, rows.shape)
    columns[...] = jnp.where(owner_first, scale_low, scale_own)


def finish_kernel(share, start, run, pairs, base, rows, columns, *refs):
    *terms, out = refs
    owner_first = pairs[0, 0] == lax.axis_index("src")
    out[0] = base[...] * rows[:, :1] * columns[...]
    placed(owner_first, share, start, run, terms, out.at[0], (rows, columns))


def small_call(kernel, out_shape, pairs, given, flops):
    return pl.pallas_call(
        kernel,
        out_shape=out_shape,
        in_specs=[pl.BlockSpec(memory_space=pltpu.SMEM)]
        + [pl.BlockSpec(memory_space=pltpu.VMEM)] * len(given),
        out_specs=jax.tree.map(lambda _: pl.BlockSpec(memory_space=pltpu.VMEM), out_shape),
        cost_estimate=pl.CostEstimate(
            flops=flops,
            bytes_accessed=sum(4 * x.size for x in given),
            transcendentals=0,
        ),
        compiler_params=pltpu.CompilerParams(vmem_limit_bytes=8 << 20),
    )(pairs, *given)


def place(pairs, terms, base, share, width, start, run):
    return small_call(
        functools.partial(place_kernel, share, start, run),
        pltpu.VMEM((share, width), jnp.float32),
        pairs,
        list(terms) + ([] if base is None else [base]),
        2 * share * width * 256,
    )


def scales_of(pairs, norm_own, norm_low, share):
    width = norm_own.shape[1]
    return small_call(
        functools.partial(scales_kernel, share),
        (pltpu.VMEM((share, 128), jnp.float32), pltpu.VMEM((1, width), jnp.float32)),
        pairs,
        [norm_own, norm_low],
        share * width,
    )


def finish(pairs, base, scales, terms, share, start, run):
    return small_call(
        functools.partial(finish_kernel, share, start, run),
        jax.ShapeDtypeStruct((1,) + base.shape, jnp.float32),
        pairs,
        [base, *scales, *terms],
        2 * base.size * 256,
    )


def top_kernel(block, out):
    pltpu.sync_copy(block.at[pl.ds(0, out.shape[0])], out)


def top_of(block, rows):
    return pl.pallas_call(
        top_kernel,
        out_shape=pltpu.VMEM((rows,) + block.shape[1:], block.dtype),
        in_specs=[pl.BlockSpec(memory_space=pltpu.HBM)],
        out_specs=pl.BlockSpec(memory_space=pltpu.VMEM),
        compiler_params=pltpu.CompilerParams(vmem_limit_bytes=60 << 20),
        name="top",
    )(block)


def on_device(greens, pairs, onsets):
    rows_dev, width = greens.shape
    groups = lax.axis_size("tm")
    share = width // groups
    runs = runs_of(share)
    aligned = groups == 8 and all(run % 8 == 0 and groups * run % 128 == 0 for _, run in runs)
    cut = rows_dev // HEAD

    head = from_behind(top_of(greens, cut), "src", 1)
    late = rows_dev - rows_dev // LATE
    pieces = [(cut, rows_dev, *run) for run in runs[:-1]]
    pieces += [(cut, late, *runs[-1]), (late, rows_dev, *runs[-1])]
    chosen = picks(greens, share, pieces)
    lower = []
    for block in chosen:
        lower.append(from_behind(block, "src", 1))
    own, squares = turn(onsets, greens)
    norm_own = summed(squares, "tm")
    norm_low = from_behind(norm_own, "src", 1)
    heads = picks(head, share, [(0, cut, *run) for run in runs])
    if not aligned:
        return plain_tail(pairs, own, heads, lower, norm_own[0], norm_low[0], share, runs)

    base = None
    for step, (run, top) in enumerate(zip(runs, heads)):
        if step < len(runs) - 1:
            ranges, blocks = [(0, cut), (cut, rows_dev)], [top, lower[step]]
        else:
            so_far = early(own, [(0, cut), (cut, late)], [top, lower[-2]])
            ranges, blocks = [(late, rows_dev)], [lower[-1], so_far]
        keep, give = gram(pairs, own, ranges, blocks, share, run[1])
        arrived = swapped(give, "tm", 1)
        mine, *gives = fold(keep, arrived)
        terms = [mine]
        for m, strip in enumerate(gives, 1):
            terms.append(swapped(strip, "tm", 2 * m))
        if step < len(runs) - 1:
            base = place(pairs, terms, base, share, width, *run)
    scales = scales_of(pairs, norm_own, norm_low, share)
    return finish(pairs, base, scales, terms, share, *runs[-1])


def plain_tail(pairs, own, heads, lower, norm_own, norm_low, share, runs):
    row_group = lax.axis_index("tm")
    owner_first = pairs[0, 0] == lax.axis_index("src")
    flags = jnp.stack([owner_first.astype(jnp.int32), row_group % 2])
    parts = []
    rests = [[block] for block in lower[:-2]] + [lower[-2:]]
    for run, top, rest in zip(runs, heads, rests):
        keep, give = gram_plain(flags, own, [top, *rest], share, run[1])
        parts.append(functools.reduce(jnp.add, strips_arrived(keep, give, "tm")))
    scale_own = lax.rsqrt(norm_own + 1e-06)
    scale_low = lax.rsqrt(norm_low + 1e-06)
    scale_rows = lax.dynamic_slice_in_dim(
        jnp.where(owner_first, scale_own, scale_low), row_group * share, share, 0
    )[:, None]
    scale_cols = jnp.where(owner_first, scale_low, scale_own)[None, :]
    base = jnp.where(
        owner_first, put_back(runs, share, parts), jnp.concatenate(parts, axis=0)
    )
    return (base * scale_rows * scale_cols)[None]


def solution(mesh):
    in_specs = (P("tm", "src"), P("src", None), P())
    out_specs = P("src", "tm", None)
    return jax.shard_map(
        on_device, mesh=mesh, in_specs=in_specs, out_specs=out_specs, check_vma=False
    )
```

```python
import functools

import jax
import jax.numpy as jnp
from jax import lax
from jax.experimental import pallas as pl
from jax.experimental.pallas import tpu as pltpu
from jax.sharding import PartitionSpec as P


PARTS = (2, 2, 1, 1)
HEAD = 8
LATE = 8


def from_behind(value, axis, by):
    length = lax.axis_size(axis)
    return lax.ppermute(value, axis, [(i, (i + by) % length) for i in range(length)])


def swapped(value, axis, bits):
    length = lax.axis_size(axis)
    return lax.ppermute(value, axis, [(i, i ^ bits) for i in range(length)])


def summed(value, axis):
    bits = 1
    while bits < lax.axis_size(axis):
        value = plus(value, swapped(value, axis, bits))
        bits *= 2
    return value


def split(strips, bit):
    halves = strips.reshape((strips.shape[0] // 2, 2) + strips.shape[1:])
    keep = lax.dynamic_index_in_dim(halves, bit, 1, keepdims=False)
    give = lax.dynamic_index_in_dim(halves, 1 - bit, 1, keepdims=False)
    return keep, give


def strips_arrived(keep, give, axis):
    me = lax.axis_index(axis) // 2
    bits = 1
    strips = keep + swapped(give, axis, bits)
    while strips.shape[0] > 4:
        keep, give = split(strips, me % 2)
        bits *= 2
        me = me // 2
        strips = keep + swapped(give, axis, bits)
    bits *= 2
    terms = [lax.dynamic_index_in_dim(strips, me, 0, keepdims=False)]
    for m in range(1, strips.shape[0]):
        give = lax.dynamic_index_in_dim(strips, me ^ m, 0, keepdims=False)
        terms.append(swapped(give, axis, bits * m))
    return terms


def runs_of(share):
    whole = sum(PARTS)
    if share % whole:
        return [(0, share)]
    unit = share // whole
    runs, start = [], 0
    for part in PARTS:
        runs.append((start, part * unit))
        start += part * unit
    return runs


def picker(width, share, start, run):
    picked = width // share * run
    q = lax.broadcasted_iota(jnp.int32, (width, picked), 1)
    source = lax.broadcasted_iota(jnp.int32, (width, picked), 0)
    return (q // run) * share + start + q % run == source


def picks_kernel(share, pieces, block, *outs):
    width = block.shape[1]
    for (low, high, start, run), out in zip(pieces, outs):
        order = picker(width, share, start, run).astype(jnp.float32).astype(jnp.bfloat16)
        out[...] = jnp.dot(
            block[low:high, :], order, preferred_element_type=jnp.float32
        ).astype(jnp.bfloat16)


def picks(block, share, pieces):
    width = block.shape[1]
    groups = width // share
    return pl.pallas_call(
        functools.partial(picks_kernel, share, pieces),
        out_shape=[
            pltpu.VMEM((high - low, groups * run), jnp.bfloat16) for low, high, _, run in pieces
        ],
        in_specs=[pl.BlockSpec(memory_space=pltpu.VMEM)],
        out_specs=[pl.BlockSpec(memory_space=pltpu.VMEM) for _ in pieces],
        cost_estimate=pl.CostEstimate(
            flops=2 * block.size * width, bytes_accessed=4 * block.size, transcendentals=0
        ),
        compiler_params=pltpu.CompilerParams(vmem_limit_bytes=55 << 20),
        name="picks",
    )(block)


def turn_kernel(step, onsets, block, turned, squares):
    rows, width = block.shape
    owner = lax.axis_index("src")
    blocks = lax.axis_size("src")
    top_row = lax.axis_index("tm") * rows
    own_first = onsets[owner] - top_row
    both_first = (
        jnp.maximum(onsets[owner], onsets[lax.rem(owner + blocks - 1, blocks)]) - top_row
    )
    total = jnp.zeros((1, width), jnp.float32)
    for top in range(0, rows, step):
        piece = block[top : top + step, :]
        ids = lax.broadcasted_iota(jnp.int32, (step, width), 0) + top
        wide = jnp.where(ids >= own_first, piece.astype(jnp.float32), 0.0)
        total = total + jnp.sum(wide * wide, axis=0, keepdims=True)
        shown = jnp.where(ids >= both_first, piece.astype(jnp.float32), 0.0)
        turned[:, top : top + step] = shown.T.astype(jnp.bfloat16)
    squares[...] = total


def turn(onsets, block):
    rows, width = block.shape
    step = 128 if rows % 128 == 0 else rows
    return pl.pallas_call(
        functools.partial(turn_kernel, step),
        out_shape=(
            pltpu.VMEM((width, rows), jnp.bfloat16),
            pltpu.VMEM((1, width), jnp.float32),
        ),
        in_specs=[pl.BlockSpec(memory_space=pltpu.SMEM), pl.BlockSpec(memory_space=pltpu.VMEM)],
        out_specs=(pl.BlockSpec(memory_space=pltpu.VMEM),) * 2,
        cost_estimate=pl.CostEstimate(
            flops=4 * block.size, bytes_accessed=4 * block.size, transcendentals=0
        ),
        compiler_params=pltpu.CompilerParams(vmem_limit_bytes=53 << 20),
        name="turn",
    )(onsets, block)


def product_of(own, ranges, refs):
    return functools.reduce(
        jnp.add,
        (
            jnp.dot(own[:, low:high], ref[...], preferred_element_type=jnp.float32)
            for (low, high), ref in zip(ranges, refs)
        ),
    )


def early_kernel(ranges, own, *refs):
    *rows, out = refs
    out[...] = product_of(own, ranges, rows)


def early(own, ranges, blocks):
    columns = blocks[0].shape[1]
    return pl.pallas_call(
        functools.partial(early_kernel, ranges),
        out_shape=pltpu.VMEM((own.shape[0], columns), jnp.float32),
        in_specs=[pl.BlockSpec(memory_space=pltpu.VMEM)] * (1 + len(blocks)),
        out_specs=pl.BlockSpec(memory_space=pltpu.VMEM),
        cost_estimate=pl.CostEstimate(
            flops=2 * own.size * columns, bytes_accessed=2 * own.size, transcendentals=0
        ),
        compiler_params=pltpu.CompilerParams(vmem_limit_bytes=16 << 20),
        name="early",
    )(own, *blocks)


def gram_kernel(share, run, ranges, pairs, own, *refs):
    *rows, keep, give, part = refs
    columns = rows[0].shape[1]
    groups = keep.shape[0] * 2
    bit = lax.rem(lax.axis_index("tm"), 2)
    owner_first = pairs[0, 0] == lax.axis_index("src")
    product = product_of(own, ranges, rows)
    if len(rows) > len(ranges):
        product = product + rows[-1][...]

    @pl.when(owner_first)
    def _():
        part[...] = product
        for pair in range(groups // 2):
            for target, odd in ((keep, bit), (give, 1 - bit)):
                top = (2 * pair + odd) * share
                for piece in range(share // run):
                    rows = pl.ds(pl.multiple_of(top + piece * run, 8), run)
                    target[pair, :, piece * columns : (piece + 1) * columns] = part[rows, :]

    @pl.when(jnp.logical_not(owner_first))
    def _():
        turned = product.T
        for pair in range(groups // 2):
            even = turned[2 * pair * run : (2 * pair + 1) * run, :]
            uneven = turned[(2 * pair + 1) * run : (2 * pair + 2) * run, :]
            keep[pair] = jnp.where(bit == 0, even, uneven)
            give[pair] = jnp.where(bit == 0, uneven, even)


def gram(pairs, own, ranges, blocks, share, run):
    width = own.shape[0]
    groups = width // share
    half = pltpu.VMEM((groups // 2, run, width), jnp.float32)
    columns = groups * run
    return pl.pallas_call(
        functools.partial(gram_kernel, share, run, ranges),
        out_shape=(half, half),
        in_specs=[pl.BlockSpec(memory_space=pltpu.SMEM)]
        + [pl.BlockSpec(memory_space=pltpu.VMEM)] * (1 + len(blocks)),
        out_specs=(pl.BlockSpec(memory_space=pltpu.VMEM),) * 2,
        scratch_shapes=[pltpu.VMEM((width, columns), jnp.float32)],
        cost_estimate=pl.CostEstimate(
            flops=2 * own.size * columns, bytes_accessed=2 * own.size, transcendentals=0
        ),
        compiler_params=pltpu.CompilerParams(vmem_limit_bytes=16 << 20),
        name="gram",
    )(pairs, own, *blocks)


def gram_plain(flags, own, blocks, share, run):
    width = own.shape[0]
    groups = width // share
    columns = groups * run
    block = jnp.concatenate(blocks, axis=0)
    product = jnp.dot(own, block, preferred_element_type=jnp.float32)
    strips = jnp.where(
        flags[0] == 1,
        product.reshape(groups, share // run, run, columns)
        .transpose(0, 2, 1, 3)
        .reshape(groups, run, width),
        product.T.reshape(groups, run, width),
    )
    return split(strips, flags[1])


def put_back(runs, share, parts):
    width = parts[0].shape[1]
    total = jnp.zeros((share, width), jnp.float32)
    for (start, run), part in zip(runs, parts):
        columns = width // share * run
        spread = (
            part.reshape(run, share // run, columns).transpose(1, 0, 2).reshape(share, columns)
        )
        total = total + lax.dot_general(
            spread,
            picker(width, share, start, run).astype(jnp.float32),
            (((1,), (1,)), ((), ())),
            precision=lax.Precision.HIGHEST,
            preferred_element_type=jnp.float32,
        )
    return total


def fold_kernel(keep, arrived, mine, *gives):
    me = lax.axis_index("tm") // 2
    mine[...] = keep[me] + arrived[me]
    for m, give in enumerate(gives, 1):
        give[...] = keep[me ^ m] + arrived[me ^ m]


def fold(keep, arrived):
    strip = pltpu.VMEM(keep.shape[1:], jnp.float32)
    return pl.pallas_call(
        fold_kernel,
        out_shape=[strip] * keep.shape[0],
        in_specs=[pl.BlockSpec(memory_space=pltpu.VMEM)] * 2,
        out_specs=[pl.BlockSpec(memory_space=pltpu.VMEM)] * keep.shape[0],
        cost_estimate=pl.CostEstimate(
            flops=keep.size, bytes_accessed=12 * keep.size, transcendentals=0
        ),
        compiler_params=pltpu.CompilerParams(vmem_limit_bytes=8 << 20),
        name="fold",
    )(keep, arrived)


def plus_kernel(a, b, out):
    out[...] = a[...] + b[...]


def plus(a, b):
    return pl.pallas_call(
        plus_kernel,
        out_shape=pltpu.VMEM(a.shape, a.dtype),
        in_specs=[pl.BlockSpec(memory_space=pltpu.VMEM)] * 2,
        out_specs=pl.BlockSpec(memory_space=pltpu.VMEM),
        compiler_params=pltpu.CompilerParams(vmem_limit_bytes=1 << 20),
        name="plus",
    )(a, b)


def placed(owner_first, share, start, run, terms, total, scales=None):
    width = total.shape[1]
    columns = width // share * run
    part = terms[0][...]
    for term in terms[1:]:
        part = part + term[...]

    @pl.when(owner_first)
    def _():
        spread = jnp.concatenate(
            [part[:, n * columns : (n + 1) * columns] for n in range(share // run)], axis=0
        )
        left = spread * 0.0625
        pieces = []
        for _ in range(3):
            pieces.append(left.astype(jnp.bfloat16))
            left = left - pieces[-1].astype(jnp.float32)
        q = lax.broadcasted_iota(jnp.int32, (columns, width), 0)
        source = lax.broadcasted_iota(jnp.int32, (columns, width), 1)
        order = (q // run) * share + start + q % run == source
        spots = jnp.dot(
            jnp.concatenate(pieces, axis=0),
            order.astype(jnp.float32).astype(jnp.bfloat16),
            preferred_element_type=jnp.float32,
        )
        added = (spots[:share] + spots[share : 2 * share] + spots[2 * share :]) * 16.0
        if scales is not None:
            added = added * scales[0][:, :1] * scales[1][...]
        total[...] += added

    @pl.when(jnp.logical_not(owner_first))
    def _():
        rows = part
        if scales is not None:
            rows = rows * scales[0][start : start + run, :1] * scales[1][...]
        total[start : start + run, :] = rows


def place_kernel(share, start, run, pairs, *refs):
    *terms, total = refs
    if len(terms) > 4:
        total[...] = terms.pop()[...]
    else:
        total[...] = jnp.zeros_like(total)
    placed(pairs[0, 0] == lax.axis_index("src"), share, start, run, terms, total)


def scales_kernel(share, pairs, norm_own, norm_low, rows, columns):
    width = columns.shape[1]
    owner_first = pairs[0, 0] == lax.axis_index("src")
    scale_own = lax.rsqrt(norm_own[...] + 1e-06)
    scale_low = lax.rsqrt(norm_low[...] + 1e-06)
    scale_first = jnp.where(owner_first, scale_own, scale_low)
    row = lax.broadcasted_iota(jnp.int32, (share, width), 0) + lax.axis_index("tm") * share
    column = lax.broadcasted_iota(jnp.int32, (share, width), 1)
    mine = jnp.sum(jnp.where(row == column, scale_first, 0.0), axis=1, keepdims=True)
    rows[...] = jnp.broadcast_to(mine, rows.shape)
    columns[...] = jnp.where(owner_first, scale_low, scale_own)


def finish_kernel(share, start, run, pairs, base, rows, columns, *refs):
    *terms, out = refs
    owner_first = pairs[0, 0] == lax.axis_index("src")
    out[0] = base[...] * rows[:, :1] * columns[...]
    placed(owner_first, share, start, run, terms, out.at[0], (rows, columns))


def small_call(kernel, out_shape, pairs, given, flops):
    return pl.pallas_call(
        kernel,
        out_shape=out_shape,
        in_specs=[pl.BlockSpec(memory_space=pltpu.SMEM)]
        + [pl.BlockSpec(memory_space=pltpu.VMEM)] * len(given),
        out_specs=jax.tree.map(lambda _: pl.BlockSpec(memory_space=pltpu.VMEM), out_shape),
        cost_estimate=pl.CostEstimate(
            flops=flops,
            bytes_accessed=sum(4 * x.size for x in given),
            transcendentals=0,
        ),
        compiler_params=pltpu.CompilerParams(vmem_limit_bytes=8 << 20),
    )(pairs, *given)


def place(pairs, terms, base, share, width, start, run):
    return small_call(
        functools.partial(place_kernel, share, start, run),
        pltpu.VMEM((share, width), jnp.float32),
        pairs,
        list(terms) + ([] if base is None else [base]),
        2 * share * width * 256,
    )


def scales_of(pairs, norm_own, norm_low, share):
    width = norm_own.shape[1]
    return small_call(
        functools.partial(scales_kernel, share),
        (pltpu.VMEM((share, 128), jnp.float32), pltpu.VMEM((1, width), jnp.float32)),
        pairs,
        [norm_own, norm_low],
        share * width,
    )


def finish(pairs, base, scales, terms, share, start, run):
    return small_call(
        functools.partial(finish_kernel, share, start, run),
        jax.ShapeDtypeStruct((1,) + base.shape, jnp.float32),
        pairs,
        [base, *scales, *terms],
        2 * base.size * 256,
    )


def top_kernel(block, out):
    pltpu.sync_copy(block.at[pl.ds(0, out.shape[0])], out)


def top_of(block, rows):
    return pl.pallas_call(
        top_kernel,
        out_shape=pltpu.VMEM((rows,) + block.shape[1:], block.dtype),
        in_specs=[pl.BlockSpec(memory_space=pltpu.HBM)],
        out_specs=pl.BlockSpec(memory_space=pltpu.VMEM),
        compiler_params=pltpu.CompilerParams(vmem_limit_bytes=60 << 20),
        name="top",
    )(block)


def on_device(greens, pairs, onsets):
    rows_dev, width = greens.shape
    groups = lax.axis_size("tm")
    share = width // groups
    runs = runs_of(share)
    aligned = groups == 8 and all(run % 8 == 0 and groups * run % 128 == 0 for _, run in runs)
    cut = rows_dev // HEAD

    head = from_behind(top_of(greens, cut), "src", 1)
    late = rows_dev - rows_dev // LATE
    pieces = [(cut, rows_dev, *run) for run in runs[:-1]]
    pieces += [(cut, late, *runs[-1]), (late, rows_dev, *runs[-1])]
    chosen = picks(greens, share, pieces)
    lower = []
    for block in chosen:
        lower.append(from_behind(block, "src", 1))
    own, squares = turn(onsets, greens)
    norm_own = summed(squares, "tm")
    norm_low = from_behind(norm_own, "src", 1)
    heads = picks(head, share, [(0, cut, *run) for run in runs])
    if not aligned:
        return plain_tail(pairs, own, heads, lower, norm_own[0], norm_low[0], share, runs)

    base = None
    for step, (run, top) in enumerate(zip(runs, heads)):
        if step < len(runs) - 1:
            ranges, blocks = [(0, cut), (cut, rows_dev)], [top, lower[step]]
        else:
            so_far = early(own, [(0, cut), (cut, late)], [top, lower[-2]])
            ranges, blocks = [(late, rows_dev)], [lower[-1], so_far]
        keep, give = gram(pairs, own, ranges, blocks, share, run[1])
        arrived = swapped(give, "tm", 1)
        mine, *gives = fold(keep, arrived)
        terms = [mine]
        for m, strip in enumerate(gives, 1):
            terms.append(swapped(strip, "tm", 2 * m))
        if step < len(runs) - 1:
            base = place(pairs, terms, base, share, width, *run)
    scales = scales_of(pairs, norm_own, norm_low, share)
    return finish(pairs, base, scales, terms, share, *runs[-1])


def plain_tail(pairs, own, heads, lower, norm_own, norm_low, share, runs):
    row_group = lax.axis_index("tm")
    owner_first = pairs[0, 0] == lax.axis_index("src")
    flags = jnp.stack([owner_first.astype(jnp.int32), row_group % 2])
    parts = []
    rests = [[block] for block in lower[:-2]] + [lower[-2:]]
    for run, top, rest in zip(runs, heads, rests):
        keep, give = gram_plain(flags, own, [top, *rest], share, run[1])
        parts.append(functools.reduce(jnp.add, strips_arrived(keep, give, "tm")))
    scale_own = lax.rsqrt(norm_own + 1e-06)
    scale_low = lax.rsqrt(norm_low + 1e-06)
    scale_rows = lax.dynamic_slice_in_dim(
        jnp.where(owner_first, scale_own, scale_low), row_group * share, share, 0
    )[:, None]
    scale_cols = jnp.where(owner_first, scale_low, scale_own)[None, :]
    base = jnp.where(
        owner_first, put_back(runs, share, parts), jnp.concatenate(parts, axis=0)
    )
    return (base * scale_rows * scale_cols)[None]


def solution(mesh):
    in_specs = (P("tm", "src"), P("src", None), P())
    out_specs = P("src", "tm", None)
    return jax.shard_map(
        on_device, mesh=mesh, in_specs=in_specs, out_specs=out_specs, check_vma=False
    )
```

```python
import functools

import jax
import jax.numpy as jnp
from jax import lax
from jax.experimental import pallas as pl
from jax.experimental.pallas import tpu as pltpu
from jax.sharding import PartitionSpec as P


PARTS = (2, 2, 1, 1)
HEAD = 8
LATE = 16


def from_behind(value, axis, by):
    length = lax.axis_size(axis)
    return lax.ppermute(value, axis, [(i, (i + by) % length) for i in range(length)])


def swapped(value, axis, bits):
    length = lax.axis_size(axis)
    return lax.ppermute(value, axis, [(i, i ^ bits) for i in range(length)])


def summed(value, axis):
    bits = 1
    while bits < lax.axis_size(axis):
        value = plus(value, swapped(value, axis, bits))
        bits *= 2
    return value


def split(strips, bit):
    halves = strips.reshape((strips.shape[0] // 2, 2) + strips.shape[1:])
    keep = lax.dynamic_index_in_dim(halves, bit, 1, keepdims=False)
    give = lax.dynamic_index_in_dim(halves, 1 - bit, 1, keepdims=False)
    return keep, give


def strips_arrived(keep, give, axis):
    me = lax.axis_index(axis) // 2
    bits = 1
    strips = keep + swapped(give, axis, bits)
    while strips.shape[0] > 4:
        keep, give = split(strips, me % 2)
        bits *= 2
        me = me // 2
        strips = keep + swapped(give, axis, bits)
    bits *= 2
    terms = [lax.dynamic_index_in_dim(strips, me, 0, keepdims=False)]
    for m in range(1, strips.shape[0]):
        give = lax.dynamic_index_in_dim(strips, me ^ m, 0, keepdims=False)
        terms.append(swapped(give, axis, bits * m))
    return terms


def runs_of(share):
    whole = sum(PARTS)
    if share % whole:
        return [(0, share)]
    unit = share // whole
    runs, start = [], 0
    for part in PARTS:
        runs.append((start, part * unit))
        start += part * unit
    return runs


def picker(width, share, start, run):
    picked = width // share * run
    q = lax.broadcasted_iota(jnp.int32, (width, picked), 1)
    source = lax.broadcasted_iota(jnp.int32, (width, picked), 0)
    return (q // run) * share + start + q % run == source


def picks_kernel(share, pieces, block, *outs):
    width = block.shape[1]
    for (low, high, start, run), out in zip(pieces, outs):
        order = picker(width, share, start, run).astype(jnp.float32).astype(jnp.bfloat16)
        out[...] = jnp.dot(
            block[low:high, :], order, preferred_element_type=jnp.float32
        ).astype(jnp.bfloat16)


def picks(block, share, pieces):
    width = block.shape[1]
    groups = width // share
    return pl.pallas_call(
        functools.partial(picks_kernel, share, pieces),
        out_shape=[
            pltpu.VMEM((high - low, groups * run), jnp.bfloat16) for low, high, _, run in pieces
        ],
        in_specs=[pl.BlockSpec(memory_space=pltpu.VMEM)],
        out_specs=[pl.BlockSpec(memory_space=pltpu.VMEM) for _ in pieces],
        cost_estimate=pl.CostEstimate(
            flops=2 * block.size * width, bytes_accessed=4 * block.size, transcendentals=0
        ),
        compiler_params=pltpu.CompilerParams(vmem_limit_bytes=55 << 20),
        name="picks",
    )(block)


def turn_kernel(step, onsets, block, turned, squares):
    rows, width = block.shape
    owner = lax.axis_index("src")
    blocks = lax.axis_size("src")
    top_row = lax.axis_index("tm") * rows
    own_first = onsets[owner] - top_row
    both_first = (
        jnp.maximum(onsets[owner], onsets[lax.rem(owner + blocks - 1, blocks)]) - top_row
    )
    total = jnp.zeros((1, width), jnp.float32)
    for top in range(0, rows, step):
        piece = block[top : top + step, :]
        ids = lax.broadcasted_iota(jnp.int32, (step, width), 0) + top
        wide = jnp.where(ids >= own_first, piece.astype(jnp.float32), 0.0)
        total = total + jnp.sum(wide * wide, axis=0, keepdims=True)
        shown = jnp.where(ids >= both_first, piece.astype(jnp.float32), 0.0)
        turned[:, top : top + step] = shown.T.astype(jnp.bfloat16)
    squares[...] = total


def turn(onsets, block):
    rows, width = block.shape
    step = 128 if rows % 128 == 0 else rows
    return pl.pallas_call(
        functools.partial(turn_kernel, step),
        out_shape=(
            pltpu.VMEM((width, rows), jnp.bfloat16),
            pltpu.VMEM((1, width), jnp.float32),
        ),
        in_specs=[pl.BlockSpec(memory_space=pltpu.SMEM), pl.BlockSpec(memory_space=pltpu.VMEM)],
        out_specs=(pl.BlockSpec(memory_space=pltpu.VMEM),) * 2,
        cost_estimate=pl.CostEstimate(
            flops=4 * block.size, bytes_accessed=4 * block.size, transcendentals=0
        ),
        compiler_params=pltpu.CompilerParams(vmem_limit_bytes=53 << 20),
        name="turn",
    )(onsets, block)


def product_of(own, ranges, refs):
    return functools.reduce(
        jnp.add,
        (
            jnp.dot(own[:, low:high], ref[...], preferred_element_type=jnp.float32)
            for (low, high), ref in zip(ranges, refs)
        ),
    )


def early_kernel(ranges, own, *refs):
    *rows, out = refs
    out[...] = product_of(own, ranges, rows)


def early(own, ranges, blocks):
    columns = blocks[0].shape[1]
    return pl.pallas_call(
        functools.partial(early_kernel, ranges),
        out_shape=pltpu.VMEM((own.shape[0], columns), jnp.float32),
        in_specs=[pl.BlockSpec(memory_space=pltpu.VMEM)] * (1 + len(blocks)),
        out_specs=pl.BlockSpec(memory_space=pltpu.VMEM),
        cost_estimate=pl.CostEstimate(
            flops=2 * own.size * columns, bytes_accessed=2 * own.size, transcendentals=0
        ),
        compiler_params=pltpu.CompilerParams(vmem_limit_bytes=16 << 20),
        name="early",
    )(own, *blocks)


def gram_kernel(share, run, ranges, pairs, own, *refs):
    *rows, keep, give, part = refs
    columns = rows[0].shape[1]
    groups = keep.shape[0] * 2
    bit = lax.rem(lax.axis_index("tm"), 2)
    owner_first = pairs[0, 0] == lax.axis_index("src")
    product = product_of(own, ranges, rows)
    if len(rows) > len(ranges):
        product = product + rows[-1][...]

    @pl.when(owner_first)
    def _():
        part[...] = product
        for pair in range(groups // 2):
            for target, odd in ((keep, bit), (give, 1 - bit)):
                top = (2 * pair + odd) * share
                for piece in range(share // run):
                    rows = pl.ds(pl.multiple_of(top + piece * run, 8), run)
                    target[pair, :, piece * columns : (piece + 1) * columns] = part[rows, :]

    @pl.when(jnp.logical_not(owner_first))
    def _():
        turned = product.T
        for pair in range(groups // 2):
            even = turned[2 * pair * run : (2 * pair + 1) * run, :]
            uneven = turned[(2 * pair + 1) * run : (2 * pair + 2) * run, :]
            keep[pair] = jnp.where(bit == 0, even, uneven)
            give[pair] = jnp.where(bit == 0, uneven, even)


def gram(pairs, own, ranges, blocks, share, run):
    width = own.shape[0]
    groups = width // share
    half = pltpu.VMEM((groups // 2, run, width), jnp.float32)
    columns = groups * run
    return pl.pallas_call(
        functools.partial(gram_kernel, share, run, ranges),
        out_shape=(half, half),
        in_specs=[pl.BlockSpec(memory_space=pltpu.SMEM)]
        + [pl.BlockSpec(memory_space=pltpu.VMEM)] * (1 + len(blocks)),
        out_specs=(pl.BlockSpec(memory_space=pltpu.VMEM),) * 2,
        scratch_shapes=[pltpu.VMEM((width, columns), jnp.float32)],
        cost_estimate=pl.CostEstimate(
            flops=2 * own.size * columns, bytes_accessed=2 * own.size, transcendentals=0
        ),
        compiler_params=pltpu.CompilerParams(vmem_limit_bytes=16 << 20),
        name="gram",
    )(pairs, own, *blocks)


def gram_plain(flags, own, blocks, share, run):
    width = own.shape[0]
    groups = width // share
    columns = groups * run
    block = jnp.concatenate(blocks, axis=0)
    product = jnp.dot(own, block, preferred_element_type=jnp.float32)
    strips = jnp.where(
        flags[0] == 1,
        product.reshape(groups, share // run, run, columns)
        .transpose(0, 2, 1, 3)
        .reshape(groups, run, width),
        product.T.reshape(groups, run, width),
    )
    return split(strips, flags[1])


def put_back(runs, share, parts):
    width = parts[0].shape[1]
    total = jnp.zeros((share, width), jnp.float32)
    for (start, run), part in zip(runs, parts):
        columns = width // share * run
        spread = (
            part.reshape(run, share // run, columns).transpose(1, 0, 2).reshape(share, columns)
        )
        total = total + lax.dot_general(
            spread,
            picker(width, share, start, run).astype(jnp.float32),
            (((1,), (1,)), ((), ())),
            precision=lax.Precision.HIGHEST,
            preferred_element_type=jnp.float32,
        )
    return total


def fold_kernel(keep, arrived, mine, *gives):
    me = lax.axis_index("tm") // 2
    mine[...] = keep[me] + arrived[me]
    for m, give in enumerate(gives, 1):
        give[...] = keep[me ^ m] + arrived[me ^ m]


def fold(keep, arrived):
    strip = pltpu.VMEM(keep.shape[1:], jnp.float32)
    return pl.pallas_call(
        fold_kernel,
        out_shape=[strip] * keep.shape[0],
        in_specs=[pl.BlockSpec(memory_space=pltpu.VMEM)] * 2,
        out_specs=[pl.BlockSpec(memory_space=pltpu.VMEM)] * keep.shape[0],
        cost_estimate=pl.CostEstimate(
            flops=keep.size, bytes_accessed=12 * keep.size, transcendentals=0
        ),
        compiler_params=pltpu.CompilerParams(vmem_limit_bytes=8 << 20),
        name="fold",
    )(keep, arrived)


def plus_kernel(a, b, out):
    out[...] = a[...] + b[...]


def plus(a, b):
    return pl.pallas_call(
        plus_kernel,
        out_shape=pltpu.VMEM(a.shape, a.dtype),
        in_specs=[pl.BlockSpec(memory_space=pltpu.VMEM)] * 2,
        out_specs=pl.BlockSpec(memory_space=pltpu.VMEM),
        compiler_params=pltpu.CompilerParams(vmem_limit_bytes=1 << 20),
        name="plus",
    )(a, b)


def spots_of(share, start, run, width):
    columns = width // share * run
    q = lax.broadcasted_iota(jnp.int32, (columns, width), 0)
    source = lax.broadcasted_iota(jnp.int32, (columns, width), 1)
    order = (q // run) * share + start + q % run == source
    return order.astype(jnp.float32).astype(jnp.bfloat16)


def placed(owner_first, share, start, run, terms, total, scales=None):
    width = total.shape[1]
    columns = width // share * run
    part = terms[0][...]
    for term in terms[1:]:
        part = part + term[...]

    @pl.when(owner_first)
    def _():
        spread = jnp.concatenate(
            [part[:, n * columns : (n + 1) * columns] for n in range(share // run)], axis=0
        )
        left = spread * 0.0625
        pieces = []
        for _ in range(3):
            pieces.append(left.astype(jnp.bfloat16))
            left = left - pieces[-1].astype(jnp.float32)
        spots = jnp.dot(
            jnp.concatenate(pieces, axis=0),
            spots_of(share, start, run, width) if scales is None else scales[2][...],
            preferred_element_type=jnp.float32,
        )
        added = (spots[:share] + spots[share : 2 * share] + spots[2 * share :]) * 16.0
        if scales is not None:
            added = added * scales[0][:, :1] * scales[1][...]
        total[...] += added

    @pl.when(jnp.logical_not(owner_first))
    def _():
        rows = part
        if scales is not None:
            rows = rows * scales[0][start : start + run, :1] * scales[1][...]
        total[start : start + run, :] = rows


def place_kernel(share, start, run, given, pairs, *refs):
    *refs, total = refs
    owner_first = pairs[0, 0] == lax.axis_index("src")
    total[...] = refs[4][...] if given else jnp.zeros_like(total)
    placed(owner_first, share, start, run, refs[:4], total)
    if given > 1:
        total[...] = total[...] * refs[5][:, :1] * refs[6][...]


def scales_kernel(share, start, run, pairs, norm_own, norm_low, rows, columns, spots):
    width = columns.shape[1]
    owner_first = pairs[0, 0] == lax.axis_index("src")
    scale_own = lax.rsqrt(norm_own[...] + 1e-06)
    scale_low = lax.rsqrt(norm_low[...] + 1e-06)
    scale_first = jnp.where(owner_first, scale_own, scale_low)
    row = lax.broadcasted_iota(jnp.int32, (share, width), 0) + lax.axis_index("tm") * share
    column = lax.broadcasted_iota(jnp.int32, (share, width), 1)
    mine = jnp.sum(jnp.where(row == column, scale_first, 0.0), axis=1, keepdims=True)
    rows[...] = jnp.broadcast_to(mine, rows.shape)
    columns[...] = jnp.where(owner_first, scale_low, scale_own)
    spots[...] = spots_of(share, start, run, width)


def finish_kernel(share, start, run, pairs, base, rows, columns, spots, *refs):
    *terms, out = refs
    owner_first = pairs[0, 0] == lax.axis_index("src")
    out[0] = base[...]
    placed(owner_first, share, start, run, terms, out.at[0], (rows, columns, spots))


def small_call(kernel, out_shape, pairs, given, flops):
    return pl.pallas_call(
        kernel,
        out_shape=out_shape,
        in_specs=[pl.BlockSpec(memory_space=pltpu.SMEM)]
        + [pl.BlockSpec(memory_space=pltpu.VMEM)] * len(given),
        out_specs=jax.tree.map(lambda _: pl.BlockSpec(memory_space=pltpu.VMEM), out_shape),
        cost_estimate=pl.CostEstimate(
            flops=flops,
            bytes_accessed=sum(4 * x.size for x in given),
            transcendentals=0,
        ),
        compiler_params=pltpu.CompilerParams(vmem_limit_bytes=8 << 20),
    )(pairs, *given)


def place(pairs, terms, base, scales, share, width, start, run):
    given = [] if base is None else [base]
    given += list(scales[:2])
    return small_call(
        functools.partial(place_kernel, share, start, run, len(given)),
        pltpu.VMEM((share, width), jnp.float32),
        pairs,
        list(terms) + given,
        2 * share * width * 256,
    )


def scales_of(pairs, norm_own, norm_low, share, start, run):
    width = norm_own.shape[1]
    return small_call(
        functools.partial(scales_kernel, share, start, run),
        (
            pltpu.VMEM((share, 128), jnp.float32),
            pltpu.VMEM((1, width), jnp.float32),
            pltpu.VMEM((width // share * run, width), jnp.bfloat16),
        ),
        pairs,
        [norm_own, norm_low],
        share * width,
    )


def finish(pairs, base, scales, terms, share, start, run):
    return small_call(
        functools.partial(finish_kernel, share, start, run),
        jax.ShapeDtypeStruct((1,) + base.shape, jnp.float32),
        pairs,
        [base, *scales, *terms],
        2 * base.size * 256,
    )


def top_kernel(block, out):
    pltpu.sync_copy(block.at[pl.ds(0, out.shape[0])], out)


def top_of(block, rows):
    return pl.pallas_call(
        top_kernel,
        out_shape=pltpu.VMEM((rows,) + block.shape[1:], block.dtype),
        in_specs=[pl.BlockSpec(memory_space=pltpu.HBM)],
        out_specs=pl.BlockSpec(memory_space=pltpu.VMEM),
        compiler_params=pltpu.CompilerParams(vmem_limit_bytes=60 << 20),
        name="top",
    )(block)


def on_device(greens, pairs, onsets):
    rows_dev, width = greens.shape
    groups = lax.axis_size("tm")
    share = width // groups
    runs = runs_of(share)
    aligned = groups == 8 and all(run % 8 == 0 and groups * run % 128 == 0 for _, run in runs)
    cut = rows_dev // HEAD

    head = from_behind(top_of(greens, cut), "src", 1)
    late = rows_dev - rows_dev // LATE
    pieces = [(cut, rows_dev, *run) for run in runs[:-1]]
    pieces += [(cut, late, *runs[-1]), (late, rows_dev, *runs[-1])]
    chosen = picks(greens, share, pieces)
    lower = []
    for block in chosen:
        lower.append(from_behind(block, "src", 1))
    own, squares = turn(onsets, greens)
    norm_own = summed(squares, "tm")
    norm_low = from_behind(norm_own, "src", 1)
    heads = picks(head, share, [(0, cut, *run) for run in runs])
    if not aligned:
        return plain_tail(pairs, own, heads, lower, norm_own[0], norm_low[0], share, runs)

    scales = scales_of(pairs, norm_own, norm_low, share, *runs[-1])
    base = None
    for step, (run, top) in enumerate(zip(runs, heads)):
        if step < len(runs) - 1:
            ranges, blocks = [(0, cut), (cut, rows_dev)], [top, lower[step]]
        else:
            so_far = early(own, [(0, cut), (cut, late)], [top, lower[-2]])
            ranges, blocks = [(late, rows_dev)], [lower[-1], so_far]
        keep, give = gram(pairs, own, ranges, blocks, share, run[1])
        arrived = swapped(give, "tm", 1)
        mine, *gives = fold(keep, arrived)
        terms = [mine]
        for m, strip in enumerate(gives, 1):
            terms.append(swapped(strip, "tm", 2 * m))
        if step < len(runs) - 1:
            used = scales if step == len(runs) - 2 else ()
            base = place(pairs, terms, base, used, share, width, *run)
    return finish(pairs, base, scales, terms, share, *runs[-1])


def plain_tail(pairs, own, heads, lower, norm_own, norm_low, share, runs):
    row_group = lax.axis_index("tm")
    owner_first = pairs[0, 0] == lax.axis_index("src")
    flags = jnp.stack([owner_first.astype(jnp.int32), row_group % 2])
    parts = []
    rests = [[block] for block in lower[:-2]] + [lower[-2:]]
    for run, top, rest in zip(runs, heads, rests):
        keep, give = gram_plain(flags, own, [top, *rest], share, run[1])
        parts.append(functools.reduce(jnp.add, strips_arrived(keep, give, "tm")))
    scale_own = lax.rsqrt(norm_own + 1e-06)
    scale_low = lax.rsqrt(norm_low + 1e-06)
    scale_rows = lax.dynamic_slice_in_dim(
        jnp.where(owner_first, scale_own, scale_low), row_group * share, share, 0
    )[:, None]
    scale_cols = jnp.where(owner_first, scale_low, scale_own)[None, :]
    base = jnp.where(
        owner_first, put_back(runs, share, parts), jnp.concatenate(parts, axis=0)
    )
    return (base * scale_rows * scale_cols)[None]


def solution(mesh):
    in_specs = (P("tm", "src"), P("src", None), P())
    out_specs = P("src", "tm", None)
    return jax.shard_map(
        on_device, mesh=mesh, in_specs=in_specs, out_specs=out_specs, check_vma=False
    )
```

```python
import functools

import jax
import jax.numpy as jnp
from jax import lax
from jax.experimental import pallas as pl
from jax.experimental.pallas import tpu as pltpu
from jax.sharding import PartitionSpec as P


PARTS = (2, 2, 1, 1)
HEAD = 8
LATE = 8
LANES = 128
TOPS = 4


def from_behind(value, axis, by):
    length = lax.axis_size(axis)
    return lax.ppermute(value, axis, [(i, (i + by) % length) for i in range(length)])


def swapped(value, axis, bits):
    length = lax.axis_size(axis)
    return lax.ppermute(value, axis, [(i, i ^ bits) for i in range(length)])


def summed(value, axis):
    bits = 1
    while bits < lax.axis_size(axis):
        value = plus(value, swapped(value, axis, bits))
        bits *= 2
    return value


def split(strips, bit):
    halves = strips.reshape((strips.shape[0] // 2, 2) + strips.shape[1:])
    keep = lax.dynamic_index_in_dim(halves, bit, 1, keepdims=False)
    give = lax.dynamic_index_in_dim(halves, 1 - bit, 1, keepdims=False)
    return keep, give


def strips_arrived(keep, give, axis):
    me = lax.axis_index(axis) // 2
    bits = 1
    strips = keep + swapped(give, axis, bits)
    while strips.shape[0] > 4:
        keep, give = split(strips, me % 2)
        bits *= 2
        me = me // 2
        strips = keep + swapped(give, axis, bits)
    bits *= 2
    terms = [lax.dynamic_index_in_dim(strips, me, 0, keepdims=False)]
    for m in range(1, strips.shape[0]):
        give = lax.dynamic_index_in_dim(strips, me ^ m, 0, keepdims=False)
        terms.append(swapped(give, axis, bits * m))
    return terms


def runs_of(share):
    whole = sum(PARTS)
    if share % whole:
        return [(0, share)]
    unit = share // whole
    runs, start = [], 0
    for part in PARTS:
        runs.append((start, part * unit))
        start += part * unit
    return runs


def picker(width, share, start, run):
    picked = width // share * run
    q = lax.broadcasted_iota(jnp.int32, (width, picked), 1)
    source = lax.broadcasted_iota(jnp.int32, (width, picked), 0)
    return (q // run) * share + start + q % run == source


def picks_kernel(share, pieces, block, *outs):
    width = block.shape[1]
    for (low, high, start, run), out in zip(pieces, outs):
        order = picker(width, share, start, run).astype(jnp.float32).astype(jnp.bfloat16)
        out[...] = jnp.dot(
            block[low:high, :], order, preferred_element_type=jnp.float32
        ).astype(jnp.bfloat16)


def picks(block, share, pieces):
    width = block.shape[1]
    groups = width // share
    return pl.pallas_call(
        functools.partial(picks_kernel, share, pieces),
        out_shape=[
            pltpu.VMEM((high - low, groups * run), jnp.bfloat16) for low, high, _, run in pieces
        ],
        in_specs=[pl.BlockSpec(memory_space=pltpu.VMEM)],
        out_specs=[pl.BlockSpec(memory_space=pltpu.VMEM) for _ in pieces],
        cost_estimate=pl.CostEstimate(
            flops=2 * block.size * width, bytes_accessed=4 * block.size, transcendentals=0
        ),
        compiler_params=pltpu.CompilerParams(vmem_limit_bytes=55 << 20),
        name="picks",
    )(block)


def turn_kernel(step, onsets, block, turned, squares):
    rows, width = block.shape
    owner = lax.axis_index("src")
    blocks = lax.axis_size("src")
    top_row = lax.axis_index("tm") * rows
    own_first = onsets[owner] - top_row
    both_first = (
        jnp.maximum(onsets[owner], onsets[lax.rem(owner + blocks - 1, blocks)]) - top_row
    )
    total = jnp.zeros((1, width), jnp.float32)
    for top in range(0, rows, step):
        piece = block[top : top + step, :]
        ids = lax.broadcasted_iota(jnp.int32, (step, width), 0) + top
        wide = jnp.where(ids >= own_first, piece.astype(jnp.float32), 0.0)
        total = total + jnp.sum(wide * wide, axis=0, keepdims=True)
        shown = jnp.where(ids >= both_first, piece.astype(jnp.float32), 0.0)
        turned[:, top : top + step] = shown.T.astype(jnp.bfloat16)
    squares[...] = total


def turn(onsets, block):
    rows, width = block.shape
    step = 128 if rows % 128 == 0 else rows
    return pl.pallas_call(
        functools.partial(turn_kernel, step),
        out_shape=(
            pltpu.VMEM((width, rows), jnp.bfloat16),
            pltpu.VMEM((1, width), jnp.float32),
        ),
        in_specs=[pl.BlockSpec(memory_space=pltpu.SMEM), pl.BlockSpec(memory_space=pltpu.VMEM)],
        out_specs=(pl.BlockSpec(memory_space=pltpu.VMEM),) * 2,
        cost_estimate=pl.CostEstimate(
            flops=4 * block.size, bytes_accessed=4 * block.size, transcendentals=0
        ),
        compiler_params=pltpu.CompilerParams(vmem_limit_bytes=53 << 20),
        name="turn",
    )(onsets, block)


def product_of(own, ranges, refs):
    return functools.reduce(
        jnp.add,
        (
            jnp.dot(own[:, low:high], ref[...], preferred_element_type=jnp.float32)
            for (low, high), ref in zip(ranges, refs)
        ),
    )


def early_kernel(ranges, own, *refs):
    *rows, out = refs
    out[...] = product_of(own, ranges, rows)


def early(own, ranges, blocks):
    columns = blocks[0].shape[1]
    return pl.pallas_call(
        functools.partial(early_kernel, ranges),
        out_shape=pltpu.VMEM((own.shape[0], columns), jnp.float32),
        in_specs=[pl.BlockSpec(memory_space=pltpu.VMEM)] * (1 + len(blocks)),
        out_specs=pl.BlockSpec(memory_space=pltpu.VMEM),
        cost_estimate=pl.CostEstimate(
            flops=2 * own.size * columns, bytes_accessed=2 * own.size, transcendentals=0
        ),
        compiler_params=pltpu.CompilerParams(vmem_limit_bytes=16 << 20),
        name="early",
    )(own, *blocks)


def gram_kernel(share, run, ranges, pairs, own, *refs):
    *rows, keep, give, part = refs
    columns = rows[0].shape[1]
    groups = keep.shape[0] * 2
    bit = lax.rem(lax.axis_index("tm"), 2)
    owner_first = pairs[0, 0] == lax.axis_index("src")
    product = product_of(own, ranges, rows)
    if len(rows) > len(ranges):
        product = product + rows[-1][...]

    @pl.when(owner_first)
    def _():
        part[...] = product
        for pair in range(groups // 2):
            for target, odd in ((keep, bit), (give, 1 - bit)):
                top = (2 * pair + odd) * share
                for piece in range(share // run):
                    rows = pl.ds(pl.multiple_of(top + piece * run, 8), run)
                    target[pair, :, piece * columns : (piece + 1) * columns] = part[rows, :]

    @pl.when(jnp.logical_not(owner_first))
    def _():
        turned = product.T
        for pair in range(groups // 2):
            even = turned[2 * pair * run : (2 * pair + 1) * run, :]
            uneven = turned[(2 * pair + 1) * run : (2 * pair + 2) * run, :]
            keep[pair] = jnp.where(bit == 0, even, uneven)
            give[pair] = jnp.where(bit == 0, uneven, even)


def gram(pairs, own, ranges, blocks, share, run):
    width = own.shape[0]
    groups = width // share
    half = pltpu.VMEM((groups // 2, run, width), jnp.float32)
    columns = groups * run
    return pl.pallas_call(
        functools.partial(gram_kernel, share, run, ranges),
        out_shape=(half, half),
        in_specs=[pl.BlockSpec(memory_space=pltpu.SMEM)]
        + [pl.BlockSpec(memory_space=pltpu.VMEM)] * (1 + len(blocks)),
        out_specs=(pl.BlockSpec(memory_space=pltpu.VMEM),) * 2,
        scratch_shapes=[pltpu.VMEM((width, columns), jnp.float32)],
        cost_estimate=pl.CostEstimate(
            flops=2 * own.size * columns, bytes_accessed=2 * own.size, transcendentals=0
        ),
        compiler_params=pltpu.CompilerParams(vmem_limit_bytes=16 << 20),
        name="gram",
    )(pairs, own, *blocks)


def gram_plain(flags, own, blocks, share, run):
    width = own.shape[0]
    groups = width // share
    columns = groups * run
    block = jnp.concatenate(blocks, axis=0)
    product = jnp.dot(own, block, preferred_element_type=jnp.float32)
    strips = jnp.where(
        flags[0] == 1,
        product.reshape(groups, share // run, run, columns)
        .transpose(0, 2, 1, 3)
        .reshape(groups, run, width),
        product.T.reshape(groups, run, width),
    )
    return split(strips, flags[1])


def put_back(runs, share, parts):
    width = parts[0].shape[1]
    total = jnp.zeros((share, width), jnp.float32)
    for (start, run), part in zip(runs, parts):
        columns = width // share * run
        spread = (
            part.reshape(run, share // run, columns).transpose(1, 0, 2).reshape(share, columns)
        )
        total = total + lax.dot_general(
            spread,
            picker(width, share, start, run).astype(jnp.float32),
            (((1,), (1,)), ((), ())),
            precision=lax.Precision.HIGHEST,
            preferred_element_type=jnp.float32,
        )
    return total


def fold_kernel(keep, arrived, mine, *gives):
    me = lax.axis_index("tm") // 2
    mine[...] = keep[me] + arrived[me]
    for m, give in enumerate(gives, 1):
        give[...] = keep[me ^ m] + arrived[me ^ m]


def fold(keep, arrived):
    strip = pltpu.VMEM(keep.shape[1:], jnp.float32)
    return pl.pallas_call(
        fold_kernel,
        out_shape=[strip] * keep.shape[0],
        in_specs=[pl.BlockSpec(memory_space=pltpu.VMEM)] * 2,
        out_specs=[pl.BlockSpec(memory_space=pltpu.VMEM)] * keep.shape[0],
        cost_estimate=pl.CostEstimate(
            flops=keep.size, bytes_accessed=12 * keep.size, transcendentals=0
        ),
        compiler_params=pltpu.CompilerParams(vmem_limit_bytes=8 << 20),
        name="fold",
    )(keep, arrived)


def plus_kernel(a, b, out):
    out[...] = a[...] + b[...]


def plus(a, b):
    return pl.pallas_call(
        plus_kernel,
        out_shape=pltpu.VMEM(a.shape, a.dtype),
        in_specs=[pl.BlockSpec(memory_space=pltpu.VMEM)] * 2,
        out_specs=pl.BlockSpec(memory_space=pltpu.VMEM),
        compiler_params=pltpu.CompilerParams(vmem_limit_bytes=1 << 20),
        name="plus",
    )(a, b)


def placed(owner_first, share, start, run, terms, total, scales=None):
    width = total.shape[1]
    columns = width // share * run
    part = terms[0][...]
    for term in terms[1:]:
        part = part + term[...]

    @pl.when(owner_first)
    def _():
        spread = jnp.concatenate(
            [part[:, n * columns : (n + 1) * columns] for n in range(share // run)], axis=0
        )
        lane = lax.broadcasted_iota(jnp.int32, (share, LANES), 1)
        for strip in range(width // share):
            source, target = strip * run, strip * share + start
            piece = spread[:, source // LANES * LANES : (source // LANES + 1) * LANES]
            shift = (target - source) % LANES
            if shift:
                piece = pltpu.roll(piece, shift, 1)
            tile = slice(target // LANES * LANES, (target // LANES + 1) * LANES)
            if scales is not None:
                piece = piece * scales[0][:, :1] * scales[1][:, tile]
            first = target % LANES
            inside = (lane >= first) & (lane < first + run)
            total[:, tile] = jnp.where(inside, piece, total[:, tile])

    @pl.when(jnp.logical_not(owner_first))
    def _():
        rows = part
        if scales is not None:
            rows = rows * scales[0][start : start + run, :1] * scales[1][...]
        total[start : start + run, :] = rows


def place_kernel(share, start, run, given, pairs, *refs):
    *refs, total = refs
    owner_first = pairs[0, 0] == lax.axis_index("src")
    total[...] = refs[4][...] if given else jnp.zeros_like(total)
    placed(owner_first, share, start, run, refs[:4], total)
    if given > 1:
        total[...] = total[...] * refs[5][:, :1] * refs[6][...]


def scales_kernel(share, pairs, norm_own, norm_low, rows, columns):
    width = columns.shape[1]
    owner_first = pairs[0, 0] == lax.axis_index("src")
    scale_own = lax.rsqrt(norm_own[...] + 1e-06)
    scale_low = lax.rsqrt(norm_low[...] + 1e-06)
    scale_first = jnp.where(owner_first, scale_own, scale_low)
    row = lax.broadcasted_iota(jnp.int32, (share, width), 0) + lax.axis_index("tm") * share
    column = lax.broadcasted_iota(jnp.int32, (share, width), 1)
    mine = jnp.sum(jnp.where(row == column, scale_first, 0.0), axis=1, keepdims=True)
    rows[...] = jnp.broadcast_to(mine, rows.shape)
    columns[...] = jnp.where(owner_first, scale_low, scale_own)


def finish_kernel(share, start, run, pairs, base, rows, columns, *refs):
    *terms, out = refs
    owner_first = pairs[0, 0] == lax.axis_index("src")
    out[0] = base[...]
    placed(owner_first, share, start, run, terms, out.at[0], (rows, columns))


def small_call(kernel, out_shape, pairs, given, flops):
    return pl.pallas_call(
        kernel,
        out_shape=out_shape,
        in_specs=[pl.BlockSpec(memory_space=pltpu.SMEM)]
        + [pl.BlockSpec(memory_space=pltpu.VMEM)] * len(given),
        out_specs=jax.tree.map(lambda _: pl.BlockSpec(memory_space=pltpu.VMEM), out_shape),
        cost_estimate=pl.CostEstimate(
            flops=flops,
            bytes_accessed=sum(4 * x.size for x in given),
            transcendentals=0,
        ),
        compiler_params=pltpu.CompilerParams(vmem_limit_bytes=8 << 20),
    )(pairs, *given)


def place(pairs, terms, base, scales, share, width, start, run):
    given = [] if base is None else [base]
    given += list(scales)
    return small_call(
        functools.partial(place_kernel, share, start, run, len(given)),
        pltpu.VMEM((share, width), jnp.float32),
        pairs,
        list(terms) + given,
        2 * share * width * 256,
    )


def scales_of(pairs, norm_own, norm_low, share):
    width = norm_own.shape[1]
    return small_call(
        functools.partial(scales_kernel, share),
        (
            pltpu.VMEM((share, LANES), jnp.float32),
            pltpu.VMEM((1, width), jnp.float32),
        ),
        pairs,
        [norm_own, norm_low],
        share * width,
    )


def finish(pairs, base, scales, terms, share, start, run):
    return small_call(
        functools.partial(finish_kernel, share, start, run),
        jax.ShapeDtypeStruct((1,) + base.shape, jnp.float32),
        pairs,
        [base, *scales, *terms],
        2 * base.size * 256,
    )


def top_kernel(block, out, sems):
    step = out.shape[0] // TOPS
    copies = [
        pltpu.make_async_copy(
            block.at[pl.ds(n * step, step)], out.at[pl.ds(n * step, step)], sems.at[n]
        )
        for n in range(TOPS)
    ]
    for copy in copies:
        copy.start()
    for copy in copies:
        copy.wait()


def top_of(block, rows):
    return pl.pallas_call(
        top_kernel,
        out_shape=pltpu.VMEM((rows,) + block.shape[1:], block.dtype),
        in_specs=[pl.BlockSpec(memory_space=pltpu.HBM)],
        out_specs=pl.BlockSpec(memory_space=pltpu.VMEM),
        scratch_shapes=[pltpu.SemaphoreType.DMA((TOPS,))],
        compiler_params=pltpu.CompilerParams(vmem_limit_bytes=60 << 20),
        name="top",
    )(block)


def on_device(greens, pairs, onsets):
    rows_dev, width = greens.shape
    groups = lax.axis_size("tm")
    share = width // groups
    runs = runs_of(share)
    aligned = groups == 8 and all(
        run % 8 == 0
        and groups * run % LANES == 0
        and LANES % run == share % run == start % run == 0
        for start, run in runs
    )
    cut = rows_dev // HEAD

    head = from_behind(top_of(greens, cut), "src", 1)
    late = rows_dev - rows_dev // LATE
    pieces = [(cut, rows_dev, *run) for run in runs[:-1]]
    pieces += [(cut, late, *runs[-1]), (late, rows_dev, *runs[-1])]
    chosen = picks(greens, share, pieces)
    lower = []
    for block in chosen:
        lower.append(from_behind(block, "src", 1))
    own, squares = turn(onsets, greens)
    norm_own = summed(squares, "tm")
    norm_low = from_behind(norm_own, "src", 1)
    heads = picks(head, share, [(0, cut, *run) for run in runs])
    if not aligned:
        return plain_tail(pairs, own, heads, lower, norm_own[0], norm_low[0], share, runs)

    scales = scales_of(pairs, norm_own, norm_low, share)
    base = None
    for step, (run, top) in enumerate(zip(runs, heads)):
        if step < len(runs) - 1:
            ranges, blocks = [(0, cut), (cut, rows_dev)], [top, lower[step]]
        else:
            so_far = early(own, [(0, cut), (cut, late)], [top, lower[-2]])
            ranges, blocks = [(late, rows_dev)], [lower[-1], so_far]
        keep, give = gram(pairs, own, ranges, blocks, share, run[1])
        arrived = swapped(give, "tm", 1)
        mine, *gives = fold(keep, arrived)
        terms = [mine]
        for m, strip in enumerate(gives, 1):
            terms.append(swapped(strip, "tm", 2 * m))
        if step < len(runs) - 1:
            used = scales if step == len(runs) - 2 else ()
            base = place(pairs, terms, base, used, share, width, *run)
    return finish(pairs, base, scales, terms, share, *runs[-1])


def plain_tail(pairs, own, heads, lower, norm_own, norm_low, share, runs):
    row_group = lax.axis_index("tm")
    owner_first = pairs[0, 0] == lax.axis_index("src")
    flags = jnp.stack([owner_first.astype(jnp.int32), row_group % 2])
    parts = []
    rests = [[block] for block in lower[:-2]] + [lower[-2:]]
    for run, top, rest in zip(runs, heads, rests):
        keep, give = gram_plain(flags, own, [top, *rest], share, run[1])
        parts.append(functools.reduce(jnp.add, strips_arrived(keep, give, "tm")))
    scale_own = lax.rsqrt(norm_own + 1e-06)
    scale_low = lax.rsqrt(norm_low + 1e-06)
    scale_rows = lax.dynamic_slice_in_dim(
        jnp.where(owner_first, scale_own, scale_low), row_group * share, share, 0
    )[:, None]
    scale_cols = jnp.where(owner_first, scale_low, scale_own)[None, :]
    base = jnp.where(
        owner_first, put_back(runs, share, parts), jnp.concatenate(parts, axis=0)
    )
    return (base * scale_rows * scale_cols)[None]


def solution(mesh):
    in_specs = (P("tm", "src"), P("src", None), P())
    out_specs = P("src", "tm", None)
    return jax.shard_map(
        on_device, mesh=mesh, in_specs=in_specs, out_specs=out_specs, check_vma=False
    )
```

```python
import functools

import jax
import jax.numpy as jnp
from jax import lax
from jax.experimental import pallas as pl
from jax.experimental.pallas import tpu as pltpu
from jax.sharding import PartitionSpec as P


PARTS = (2, 2, 1, 1)
HEAD = 8
LATE = 8
LANES = 128
TOPS = 4


def from_behind(value, axis, by):
    length = lax.axis_size(axis)
    return lax.ppermute(value, axis, [(i, (i + by) % length) for i in range(length)])


def swapped(value, axis, bits):
    length = lax.axis_size(axis)
    return lax.ppermute(value, axis, [(i, i ^ bits) for i in range(length)])


def summed(value, axis):
    bits = 1
    while bits < lax.axis_size(axis):
        value = plus(value, swapped(value, axis, bits))
        bits *= 2
    return value


def split(strips, bit):
    halves = strips.reshape((strips.shape[0] // 2, 2) + strips.shape[1:])
    keep = lax.dynamic_index_in_dim(halves, bit, 1, keepdims=False)
    give = lax.dynamic_index_in_dim(halves, 1 - bit, 1, keepdims=False)
    return keep, give


def strips_arrived(keep, give, axis):
    me = lax.axis_index(axis) // 2
    bits = 1
    strips = keep + swapped(give, axis, bits)
    while strips.shape[0] > 4:
        keep, give = split(strips, me % 2)
        bits *= 2
        me = me // 2
        strips = keep + swapped(give, axis, bits)
    bits *= 2
    terms = [lax.dynamic_index_in_dim(strips, me, 0, keepdims=False)]
    for m in range(1, strips.shape[0]):
        give = lax.dynamic_index_in_dim(strips, me ^ m, 0, keepdims=False)
        terms.append(swapped(give, axis, bits * m))
    return terms


def runs_of(share):
    whole = sum(PARTS)
    if share % whole:
        return [(0, share)]
    unit = share // whole
    runs, start = [], 0
    for part in PARTS:
        runs.append((start, part * unit))
        start += part * unit
    return runs


def picker(width, share, start, run):
    picked = width // share * run
    q = lax.broadcasted_iota(jnp.int32, (width, picked), 1)
    source = lax.broadcasted_iota(jnp.int32, (width, picked), 0)
    return (q // run) * share + start + q % run == source


def picks_kernel(share, pieces, block, *outs):
    width = block.shape[1]
    for (low, high, start, run), out in zip(pieces, outs):
        order = picker(width, share, start, run).astype(jnp.float32).astype(jnp.bfloat16)
        out[...] = jnp.dot(
            block[low:high, :], order, preferred_element_type=jnp.float32
        ).astype(jnp.bfloat16)


def picks(block, share, pieces):
    width = block.shape[1]
    groups = width // share
    return pl.pallas_call(
        functools.partial(picks_kernel, share, pieces),
        out_shape=[
            pltpu.VMEM((high - low, groups * run), jnp.bfloat16) for low, high, _, run in pieces
        ],
        in_specs=[pl.BlockSpec(memory_space=pltpu.VMEM)],
        out_specs=[pl.BlockSpec(memory_space=pltpu.VMEM) for _ in pieces],
        cost_estimate=pl.CostEstimate(
            flops=2 * block.size * width, bytes_accessed=4 * block.size, transcendentals=0
        ),
        compiler_params=pltpu.CompilerParams(vmem_limit_bytes=55 << 20),
        name="picks",
    )(block)


def turn_kernel(step, onsets, block, turned, squares):
    rows, width = block.shape
    owner = lax.axis_index("src")
    blocks = lax.axis_size("src")
    top_row = lax.axis_index("tm") * rows
    own_first = onsets[owner] - top_row
    both_first = (
        jnp.maximum(onsets[owner], onsets[lax.rem(owner + blocks - 1, blocks)]) - top_row
    )
    total = jnp.zeros((1, width), jnp.float32)
    for top in range(0, rows, step):
        piece = block[top : top + step, :]
        ids = lax.broadcasted_iota(jnp.int32, (step, width), 0) + top
        wide = jnp.where(ids >= own_first, piece.astype(jnp.float32), 0.0)
        total = total + jnp.sum(wide * wide, axis=0, keepdims=True)
        shown = jnp.where(ids >= both_first, piece.astype(jnp.float32), 0.0)
        turned[:, top : top + step] = shown.T.astype(jnp.bfloat16)
    squares[...] = total


def turn(onsets, block):
    rows, width = block.shape
    step = 128 if rows % 128 == 0 else rows
    return pl.pallas_call(
        functools.partial(turn_kernel, step),
        out_shape=(
            pltpu.VMEM((width, rows), jnp.bfloat16),
            pltpu.VMEM((1, width), jnp.float32),
        ),
        in_specs=[pl.BlockSpec(memory_space=pltpu.SMEM), pl.BlockSpec(memory_space=pltpu.VMEM)],
        out_specs=(pl.BlockSpec(memory_space=pltpu.VMEM),) * 2,
        cost_estimate=pl.CostEstimate(
            flops=4 * block.size, bytes_accessed=4 * block.size, transcendentals=0
        ),
        compiler_params=pltpu.CompilerParams(vmem_limit_bytes=53 << 20),
        name="turn",
    )(onsets, block)


def product_of(own, ranges, refs):
    return functools.reduce(
        jnp.add,
        (
            jnp.dot(own[:, low:high], ref[...], preferred_element_type=jnp.float32)
            for (low, high), ref in zip(ranges, refs)
        ),
    )


def early_kernel(ranges, own, *refs):
    *rows, out = refs
    out[...] = product_of(own, ranges, rows)


def early(own, ranges, blocks):
    columns = blocks[0].shape[1]
    return pl.pallas_call(
        functools.partial(early_kernel, ranges),
        out_shape=pltpu.VMEM((own.shape[0], columns), jnp.float32),
        in_specs=[pl.BlockSpec(memory_space=pltpu.VMEM)] * (1 + len(blocks)),
        out_specs=pl.BlockSpec(memory_space=pltpu.VMEM),
        cost_estimate=pl.CostEstimate(
            flops=2 * own.size * columns, bytes_accessed=2 * own.size, transcendentals=0
        ),
        compiler_params=pltpu.CompilerParams(vmem_limit_bytes=16 << 20),
        name="early",
    )(own, *blocks)


def gram_kernel(share, run, ranges, flag, own, *refs):
    *rows, keep, give, part = refs
    columns = rows[0].shape[1]
    groups = keep.shape[0] * 2
    bit = lax.rem(lax.axis_index("tm"), 2)
    owner_first = flag[0] == 1
    product = product_of(own, ranges, rows)
    if len(rows) > len(ranges):
        product = product + rows[-1][...]

    @pl.when(owner_first)
    def _():
        part[...] = product
        for pair in range(groups // 2):
            for target, odd in ((keep, bit), (give, 1 - bit)):
                top = (2 * pair + odd) * share
                for piece in range(share // run):
                    rows = pl.ds(pl.multiple_of(top + piece * run, 8), run)
                    target[pair, :, piece * columns : (piece + 1) * columns] = part[rows, :]

    @pl.when(jnp.logical_not(owner_first))
    def _():
        turned = product.T
        for pair in range(groups // 2):
            even = turned[2 * pair * run : (2 * pair + 1) * run, :]
            uneven = turned[(2 * pair + 1) * run : (2 * pair + 2) * run, :]
            keep[pair] = jnp.where(bit == 0, even, uneven)
            give[pair] = jnp.where(bit == 0, uneven, even)


def gram(pairs, own, ranges, blocks, share, run):
    width = own.shape[0]
    groups = width // share
    half = pltpu.VMEM((groups // 2, run, width), jnp.float32)
    columns = groups * run
    return pl.pallas_call(
        functools.partial(gram_kernel, share, run, ranges),
        out_shape=(half, half),
        in_specs=[pl.BlockSpec(memory_space=pltpu.SMEM)]
        + [pl.BlockSpec(memory_space=pltpu.VMEM)] * (1 + len(blocks)),
        out_specs=(pl.BlockSpec(memory_space=pltpu.VMEM),) * 2,
        scratch_shapes=[pltpu.VMEM((width, columns), jnp.float32)],
        cost_estimate=pl.CostEstimate(
            flops=2 * own.size * columns, bytes_accessed=2 * own.size, transcendentals=0
        ),
        compiler_params=pltpu.CompilerParams(vmem_limit_bytes=16 << 20),
        name="gram",
    )(pairs, own, *blocks)


def gram_plain(flags, own, blocks, share, run):
    width = own.shape[0]
    groups = width // share
    columns = groups * run
    block = jnp.concatenate(blocks, axis=0)
    product = jnp.dot(own, block, preferred_element_type=jnp.float32)
    strips = jnp.where(
        flags[0] == 1,
        product.reshape(groups, share // run, run, columns)
        .transpose(0, 2, 1, 3)
        .reshape(groups, run, width),
        product.T.reshape(groups, run, width),
    )
    return split(strips, flags[1])


def put_back(runs, share, parts):
    width = parts[0].shape[1]
    total = jnp.zeros((share, width), jnp.float32)
    for (start, run), part in zip(runs, parts):
        columns = width // share * run
        spread = (
            part.reshape(run, share // run, columns).transpose(1, 0, 2).reshape(share, columns)
        )
        total = total + lax.dot_general(
            spread,
            picker(width, share, start, run).astype(jnp.float32),
            (((1,), (1,)), ((), ())),
            precision=lax.Precision.HIGHEST,
            preferred_element_type=jnp.float32,
        )
    return total


def fold_kernel(keep, arrived, mine, *gives):
    me = lax.axis_index("tm") // 2
    mine[...] = keep[me] + arrived[me]
    for m, give in enumerate(gives, 1):
        give[...] = keep[me ^ m] + arrived[me ^ m]


def fold(keep, arrived):
    strip = pltpu.VMEM(keep.shape[1:], jnp.float32)
    return pl.pallas_call(
        fold_kernel,
        out_shape=[strip] * keep.shape[0],
        in_specs=[pl.BlockSpec(memory_space=pltpu.VMEM)] * 2,
        out_specs=[pl.BlockSpec(memory_space=pltpu.VMEM)] * keep.shape[0],
        cost_estimate=pl.CostEstimate(
            flops=keep.size, bytes_accessed=12 * keep.size, transcendentals=0
        ),
        compiler_params=pltpu.CompilerParams(vmem_limit_bytes=8 << 20),
        name="fold",
    )(keep, arrived)


def flag_kernel(pairs, out):
    out[0] = jnp.where(pairs[0, 0] == lax.axis_index("src"), 1, 0)


def flag_of(pairs):
    return pl.pallas_call(
        flag_kernel,
        out_shape=pltpu.SMEM((1,), jnp.int32),
        in_specs=[pl.BlockSpec(memory_space=pltpu.SMEM)],
        out_specs=pl.BlockSpec(memory_space=pltpu.SMEM),
        compiler_params=pltpu.CompilerParams(vmem_limit_bytes=1 << 20),
        name="flag",
    )(pairs)


def across_kernel(keep, arrived, kept, given):
    bit = lax.axis_index("tm") // 2 % 2
    for n in range(kept.shape[0]):
        kept[n] = keep[2 * n + bit] + arrived[2 * n + bit]
        given[n] = keep[2 * n + 1 - bit] + arrived[2 * n + 1 - bit]


def last_kernel(keep, arrived, kept, given):
    bit = lax.axis_index("tm") // 4
    kept[...] = keep[bit] + arrived[bit]
    given[...] = keep[1 - bit] + arrived[1 - bit]


def halved(kernel, keep, arrived, shape):
    half = pltpu.VMEM(shape, jnp.float32)
    return pl.pallas_call(
        kernel,
        out_shape=[half, half],
        in_specs=[pl.BlockSpec(memory_space=pltpu.VMEM)] * 2,
        out_specs=[pl.BlockSpec(memory_space=pltpu.VMEM)] * 2,
        cost_estimate=pl.CostEstimate(
            flops=keep.size, bytes_accessed=12 * keep.size, transcendentals=0
        ),
        compiler_params=pltpu.CompilerParams(vmem_limit_bytes=8 << 20),
        name="halved",
    )(keep, arrived)


def plus_kernel(a, b, out):
    out[...] = a[...] + b[...]


def plus(a, b):
    return pl.pallas_call(
        plus_kernel,
        out_shape=pltpu.VMEM(a.shape, a.dtype),
        in_specs=[pl.BlockSpec(memory_space=pltpu.VMEM)] * 2,
        out_specs=pl.BlockSpec(memory_space=pltpu.VMEM),
        compiler_params=pltpu.CompilerParams(vmem_limit_bytes=1 << 20),
        name="plus",
    )(a, b)


def placed(owner_first, share, start, run, terms, total, scales=None):
    width = total.shape[1]
    columns = width // share * run
    part = terms[0][...]
    for term in terms[1:]:
        part = part + term[...]

    @pl.when(owner_first)
    def _():
        spread = jnp.concatenate(
            [part[:, n * columns : (n + 1) * columns] for n in range(share // run)], axis=0
        )
        lane = lax.broadcasted_iota(jnp.int32, (share, LANES), 1)
        for strip in range(width // share):
            source, target = strip * run, strip * share + start
            piece = spread[:, source // LANES * LANES : (source // LANES + 1) * LANES]
            shift = (target - source) % LANES
            if shift:
                piece = pltpu.roll(piece, shift, 1)
            tile = slice(target // LANES * LANES, (target // LANES + 1) * LANES)
            if scales is not None:
                piece = piece * scales[0][:, :1] * scales[1][:, tile]
            first = target % LANES
            inside = (lane >= first) & (lane < first + run)
            total[:, tile] = jnp.where(inside, piece, total[:, tile])

    @pl.when(jnp.logical_not(owner_first))
    def _():
        rows = part
        if scales is not None:
            rows = rows * scales[0][start : start + run, :1] * scales[1][...]
        total[start : start + run, :] = rows


def place_kernel(share, start, run, given, flag, *refs):
    *refs, total = refs
    owner_first = flag[0] == 1
    total[...] = refs[4][...] if given else jnp.zeros_like(total)
    placed(owner_first, share, start, run, refs[:4], total)
    if given > 1:
        total[...] = total[...] * refs[5][:, :1] * refs[6][...]


def scales_kernel(share, flag, norm_own, norm_low, rows, columns):
    width = columns.shape[1]
    owner_first = flag[0] == 1
    scale_own = lax.rsqrt(norm_own[...] + 1e-06)
    scale_low = lax.rsqrt(norm_low[...] + 1e-06)
    scale_first = jnp.where(owner_first, scale_own, scale_low)
    row = lax.broadcasted_iota(jnp.int32, (share, width), 0) + lax.axis_index("tm") * share
    column = lax.broadcasted_iota(jnp.int32, (share, width), 1)
    mine = jnp.sum(jnp.where(row == column, scale_first, 0.0), axis=1, keepdims=True)
    rows[...] = jnp.broadcast_to(mine, rows.shape)
    columns[...] = jnp.where(owner_first, scale_low, scale_own)


def finish_kernel(share, start, run, flag, base, rows, columns, *refs):
    *terms, out = refs
    owner_first = flag[0] == 1
    out[0] = base[...]
    placed(owner_first, share, start, run, terms, out.at[0], (rows, columns))


def small_call(kernel, out_shape, pairs, given, flops):
    return pl.pallas_call(
        kernel,
        out_shape=out_shape,
        in_specs=[pl.BlockSpec(memory_space=pltpu.SMEM)]
        + [pl.BlockSpec(memory_space=pltpu.VMEM)] * len(given),
        out_specs=jax.tree.map(lambda _: pl.BlockSpec(memory_space=pltpu.VMEM), out_shape),
        cost_estimate=pl.CostEstimate(
            flops=flops,
            bytes_accessed=sum(4 * x.size for x in given),
            transcendentals=0,
        ),
        compiler_params=pltpu.CompilerParams(vmem_limit_bytes=8 << 20),
    )(pairs, *given)


def place(pairs, terms, base, scales, share, width, start, run):
    given = [] if base is None else [base]
    given += list(scales)
    return small_call(
        functools.partial(place_kernel, share, start, run, len(given)),
        pltpu.VMEM((share, width), jnp.float32),
        pairs,
        list(terms) + given,
        2 * share * width * 256,
    )


def scales_of(pairs, norm_own, norm_low, share):
    width = norm_own.shape[1]
    return small_call(
        functools.partial(scales_kernel, share),
        (
            pltpu.VMEM((share, LANES), jnp.float32),
            pltpu.VMEM((1, width), jnp.float32),
        ),
        pairs,
        [norm_own, norm_low],
        share * width,
    )


def finish(pairs, base, scales, terms, share, start, run):
    return small_call(
        functools.partial(finish_kernel, share, start, run),
        jax.ShapeDtypeStruct((1,) + base.shape, jnp.float32),
        pairs,
        [base, *scales, *terms],
        2 * base.size * 256,
    )


def top_kernel(block, out, sems):
    step = out.shape[0] // TOPS
    copies = [
        pltpu.make_async_copy(
            block.at[pl.ds(n * step, step)], out.at[pl.ds(n * step, step)], sems.at[n]
        )
        for n in range(TOPS)
    ]
    for copy in copies:
        copy.start()
    for copy in copies:
        copy.wait()


def top_of(block, rows):
    return pl.pallas_call(
        top_kernel,
        out_shape=pltpu.VMEM((rows,) + block.shape[1:], block.dtype),
        in_specs=[pl.BlockSpec(memory_space=pltpu.HBM)],
        out_specs=pl.BlockSpec(memory_space=pltpu.VMEM),
        scratch_shapes=[pltpu.SemaphoreType.DMA((TOPS,))],
        compiler_params=pltpu.CompilerParams(vmem_limit_bytes=60 << 20),
        name="top",
    )(block)


def on_device(greens, pairs, onsets):
    rows_dev, width = greens.shape
    groups = lax.axis_size("tm")
    share = width // groups
    runs = runs_of(share)
    aligned = groups == 8 and all(
        run % 8 == 0
        and groups * run % LANES == 0
        and LANES % run == share % run == start % run == 0
        for start, run in runs
    )
    cut = rows_dev // HEAD

    head = from_behind(top_of(greens, cut), "src", 1)
    late = rows_dev - rows_dev // LATE
    pieces = [(cut, rows_dev, *run) for run in runs[:-1]]
    pieces += [(cut, late, *runs[-1]), (late, rows_dev, *runs[-1])]
    chosen = picks(greens, share, pieces)
    lower = []
    for block in chosen:
        lower.append(from_behind(block, "src", 1))
    own, squares = turn(onsets, greens)
    norm_own = summed(squares, "tm")
    norm_low = from_behind(norm_own, "src", 1)
    heads = picks(head, share, [(0, cut, *run) for run in runs])
    if not aligned:
        return plain_tail(pairs, own, heads, lower, norm_own[0], norm_low[0], share, runs)

    flag = flag_of(pairs)
    scales = scales_of(flag, norm_own, norm_low, share)
    base = None
    for step, (run, top) in enumerate(zip(runs, heads)):
        if step < len(runs) - 1:
            ranges, blocks = [(0, cut), (cut, rows_dev)], [top, lower[step]]
        else:
            so_far = early(own, [(0, cut), (cut, late)], [top, lower[-2]])
            ranges, blocks = [(late, rows_dev)], [lower[-1], so_far]
        keep, give = gram(flag, own, ranges, blocks, share, run[1])
        arrived = swapped(give, "tm", 1)
        if step == len(runs) - 1:
            strip = keep.shape[1:]
            kept, given = halved(across_kernel, keep, arrived, (2, *strip))
            arrived = swapped(given, "tm", 2)
            kept, given = halved(last_kernel, kept, arrived, strip)
            terms = [kept, swapped(given, "tm", 4)]
            break
        mine, *gives = fold(keep, arrived)
        terms = [mine]
        for m, strip in enumerate(gives, 1):
            terms.append(swapped(strip, "tm", 2 * m))
        used = scales if step == len(runs) - 2 else ()
        base = place(flag, terms, base, used, share, width, *run)
    return finish(flag, base, scales, terms, share, *runs[-1])


def plain_tail(pairs, own, heads, lower, norm_own, norm_low, share, runs):
    row_group = lax.axis_index("tm")
    owner_first = pairs[0, 0] == lax.axis_index("src")
    flags = jnp.stack([owner_first.astype(jnp.int32), row_group % 2])
    parts = []
    rests = [[block] for block in lower[:-2]] + [lower[-2:]]
    for run, top, rest in zip(runs, heads, rests):
        keep, give = gram_plain(flags, own, [top, *rest], share, run[1])
        parts.append(functools.reduce(jnp.add, strips_arrived(keep, give, "tm")))
    scale_own = lax.rsqrt(norm_own + 1e-06)
    scale_low = lax.rsqrt(norm_low + 1e-06)
    scale_rows = lax.dynamic_slice_in_dim(
        jnp.where(owner_first, scale_own, scale_low), row_group * share, share, 0
    )[:, None]
    scale_cols = jnp.where(owner_first, scale_low, scale_own)[None, :]
    base = jnp.where(
        owner_first, put_back(runs, share, parts), jnp.concatenate(parts, axis=0)
    )
    return (base * scale_rows * scale_cols)[None]


def solution(mesh):
    in_specs = (P("tm", "src"), P("src", None), P())
    out_specs = P("src", "tm", None)
    return jax.shard_map(
        on_device, mesh=mesh, in_specs=in_specs, out_specs=out_specs, check_vma=False
    )
```

```python
import functools

import jax
import jax.numpy as jnp
from jax import lax
from jax.experimental import pallas as pl
from jax.experimental.pallas import tpu as pltpu
from jax.sharding import PartitionSpec as P


PARTS = (2, 2, 1, 1)
HEAD = 8
LATE = 2
LANES = 128
TOPS = 1


def from_behind(value, axis, by):
    length = lax.axis_size(axis)
    return lax.ppermute(value, axis, [(i, (i + by) % length) for i in range(length)])


def swapped(value, axis, bits):
    length = lax.axis_size(axis)
    return lax.ppermute(value, axis, [(i, i ^ bits) for i in range(length)])


def summed(value, axis):
    bits = 1
    while bits < lax.axis_size(axis):
        value = plus(value, swapped(value, axis, bits))
        bits *= 2
    return value


def split(strips, bit):
    halves = strips.reshape((strips.shape[0] // 2, 2) + strips.shape[1:])
    keep = lax.dynamic_index_in_dim(halves, bit, 1, keepdims=False)
    give = lax.dynamic_index_in_dim(halves, 1 - bit, 1, keepdims=False)
    return keep, give


def strips_arrived(keep, give, axis):
    me = lax.axis_index(axis) // 2
    bits = 1
    strips = keep + swapped(give, axis, bits)
    while strips.shape[0] > 4:
        keep, give = split(strips, me % 2)
        bits *= 2
        me = me // 2
        strips = keep + swapped(give, axis, bits)
    bits *= 2
    terms = [lax.dynamic_index_in_dim(strips, me, 0, keepdims=False)]
    for m in range(1, strips.shape[0]):
        give = lax.dynamic_index_in_dim(strips, me ^ m, 0, keepdims=False)
        terms.append(swapped(give, axis, bits * m))
    return terms


def runs_of(share):
    whole = sum(PARTS)
    if share % whole:
        return [(0, share)]
    unit = share // whole
    runs, start = [], 0
    for part in PARTS:
        runs.append((start, part * unit))
        start += part * unit
    return runs


def picker(width, share, start, run):
    picked = width // share * run
    q = lax.broadcasted_iota(jnp.int32, (width, picked), 1)
    source = lax.broadcasted_iota(jnp.int32, (width, picked), 0)
    return (q // run) * share + start + q % run == source


def picks_kernel(share, pieces, block, *outs):
    width = block.shape[1]
    for (low, high, start, run), out in zip(pieces, outs):
        order = picker(width, share, start, run).astype(jnp.float32).astype(jnp.bfloat16)
        out[...] = jnp.dot(
            block[low:high, :], order, preferred_element_type=jnp.float32
        ).astype(jnp.bfloat16)


def picks(block, share, pieces):
    width = block.shape[1]
    groups = width // share
    return pl.pallas_call(
        functools.partial(picks_kernel, share, pieces),
        out_shape=[
            pltpu.VMEM((high - low, groups * run), jnp.bfloat16) for low, high, _, run in pieces
        ],
        in_specs=[pl.BlockSpec(memory_space=pltpu.VMEM)],
        out_specs=[pl.BlockSpec(memory_space=pltpu.VMEM) for _ in pieces],
        cost_estimate=pl.CostEstimate(
            flops=2 * block.size * width, bytes_accessed=4 * block.size, transcendentals=0
        ),
        compiler_params=pltpu.CompilerParams(vmem_limit_bytes=55 << 20),
        name="picks",
    )(block)


def turn_kernel(step, onsets, block, turned, squares):
    rows, width = block.shape
    owner = lax.axis_index("src")
    blocks = lax.axis_size("src")
    top_row = lax.axis_index("tm") * rows
    own_first = onsets[owner] - top_row
    both_first = (
        jnp.maximum(onsets[owner], onsets[lax.rem(owner + blocks - 1, blocks)]) - top_row
    )
    total = jnp.zeros((1, width), jnp.float32)
    for top in range(0, rows, step):
        piece = block[top : top + step, :]
        ids = lax.broadcasted_iota(jnp.int32, (step, width), 0) + top
        wide = jnp.where(ids >= own_first, piece.astype(jnp.float32), 0.0)
        total = total + jnp.sum(wide * wide, axis=0, keepdims=True)
        shown = jnp.where(ids >= both_first, piece.astype(jnp.float32), 0.0)
        turned[:, top : top + step] = shown.T.astype(jnp.bfloat16)
    squares[...] = total


def turn(onsets, block):
    rows, width = block.shape
    step = 128 if rows % 128 == 0 else rows
    return pl.pallas_call(
        functools.partial(turn_kernel, step),
        out_shape=(
            pltpu.VMEM((width, rows), jnp.bfloat16),
            pltpu.VMEM((1, width), jnp.float32),
        ),
        in_specs=[pl.BlockSpec(memory_space=pltpu.SMEM), pl.BlockSpec(memory_space=pltpu.VMEM)],
        out_specs=(pl.BlockSpec(memory_space=pltpu.VMEM),) * 2,
        cost_estimate=pl.CostEstimate(
            flops=4 * block.size, bytes_accessed=4 * block.size, transcendentals=0
        ),
        compiler_params=pltpu.CompilerParams(vmem_limit_bytes=53 << 20),
        name="turn",
    )(onsets, block)


def product_of(own, ranges, refs):
    return functools.reduce(
        jnp.add,
        (
            jnp.dot(own[:, low:high], ref[...], preferred_element_type=jnp.float32)
            for (low, high), ref in zip(ranges, refs)
        ),
    )


def early_kernel(ranges, own, *refs):
    *rows, out = refs
    out[...] = product_of(own, ranges, rows)


def early(own, ranges, blocks):
    columns = blocks[0].shape[1]
    return pl.pallas_call(
        functools.partial(early_kernel, ranges),
        out_shape=pltpu.VMEM((own.shape[0], columns), jnp.float32),
        in_specs=[pl.BlockSpec(memory_space=pltpu.VMEM)] * (1 + len(blocks)),
        out_specs=pl.BlockSpec(memory_space=pltpu.VMEM),
        cost_estimate=pl.CostEstimate(
            flops=2 * own.size * columns, bytes_accessed=2 * own.size, transcendentals=0
        ),
        compiler_params=pltpu.CompilerParams(vmem_limit_bytes=16 << 20),
        name="early",
    )(own, *blocks)


def gram_kernel(share, run, ranges, flag, own, *refs):
    *rows, keep, give, part = refs
    columns = rows[0].shape[1]
    groups = keep.shape[0] * 2
    bit = lax.rem(lax.axis_index("tm"), 2)
    owner_first = flag[0] == 1
    product = product_of(own, ranges, rows)
    if len(rows) > len(ranges):
        product = product + rows[-1][...]

    @pl.when(owner_first)
    def _():
        part[...] = product
        for pair in range(groups // 2):
            for target, odd in ((keep, bit), (give, 1 - bit)):
                top = (2 * pair + odd) * share
                for piece in range(share // run):
                    rows = pl.ds(pl.multiple_of(top + piece * run, 8), run)
                    target[pair, :, piece * columns : (piece + 1) * columns] = part[rows, :]

    @pl.when(jnp.logical_not(owner_first))
    def _():
        turned = product.T
        for pair in range(groups // 2):
            even = turned[2 * pair * run : (2 * pair + 1) * run, :]
            uneven = turned[(2 * pair + 1) * run : (2 * pair + 2) * run, :]
            keep[pair] = jnp.where(bit == 0, even, uneven)
            give[pair] = jnp.where(bit == 0, uneven, even)


def gram(pairs, own, ranges, blocks, share, run):
    width = own.shape[0]
    groups = width // share
    half = pltpu.VMEM((groups // 2, run, width), jnp.float32)
    columns = groups * run
    return pl.pallas_call(
        functools.partial(gram_kernel, share, run, ranges),
        out_shape=(half, half),
        in_specs=[pl.BlockSpec(memory_space=pltpu.SMEM)]
        + [pl.BlockSpec(memory_space=pltpu.VMEM)] * (1 + len(blocks)),
        out_specs=(pl.BlockSpec(memory_space=pltpu.VMEM),) * 2,
        scratch_shapes=[pltpu.VMEM((width, columns), jnp.float32)],
        cost_estimate=pl.CostEstimate(
            flops=2 * own.size * columns, bytes_accessed=2 * own.size, transcendentals=0
        ),
        compiler_params=pltpu.CompilerParams(vmem_limit_bytes=16 << 20),
        name="gram",
    )(pairs, own, *blocks)


def gram_plain(flags, own, blocks, share, run):
    width = own.shape[0]
    groups = width // share
    columns = groups * run
    block = jnp.concatenate(blocks, axis=0)
    product = jnp.dot(own, block, preferred_element_type=jnp.float32)
    strips = jnp.where(
        flags[0] == 1,
        product.reshape(groups, share // run, run, columns)
        .transpose(0, 2, 1, 3)
        .reshape(groups, run, width),
        product.T.reshape(groups, run, width),
    )
    return split(strips, flags[1])


def put_back(runs, share, parts):
    width = parts[0].shape[1]
    total = jnp.zeros((share, width), jnp.float32)
    for (start, run), part in zip(runs, parts):
        columns = width // share * run
        spread = (
            part.reshape(run, share // run, columns).transpose(1, 0, 2).reshape(share, columns)
        )
        total = total + lax.dot_general(
            spread,
            picker(width, share, start, run).astype(jnp.float32),
            (((1,), (1,)), ((), ())),
            precision=lax.Precision.HIGHEST,
            preferred_element_type=jnp.float32,
        )
    return total


def fold_kernel(keep, arrived, mine, *gives):
    me = lax.axis_index("tm") // 2
    mine[...] = keep[me] + arrived[me]
    for m, give in enumerate(gives, 1):
        give[...] = keep[me ^ m] + arrived[me ^ m]


def fold(keep, arrived):
    strip = pltpu.VMEM(keep.shape[1:], jnp.float32)
    return pl.pallas_call(
        fold_kernel,
        out_shape=[strip] * keep.shape[0],
        in_specs=[pl.BlockSpec(memory_space=pltpu.VMEM)] * 2,
        out_specs=[pl.BlockSpec(memory_space=pltpu.VMEM)] * keep.shape[0],
        cost_estimate=pl.CostEstimate(
            flops=keep.size, bytes_accessed=12 * keep.size, transcendentals=0
        ),
        compiler_params=pltpu.CompilerParams(vmem_limit_bytes=8 << 20),
        name="fold",
    )(keep, arrived)


def flag_kernel(pairs, out):
    out[0] = jnp.where(pairs[0, 0] == lax.axis_index("src"), 1, 0)


def flag_of(pairs):
    return pl.pallas_call(
        flag_kernel,
        out_shape=pltpu.SMEM((1,), jnp.int32),
        in_specs=[pl.BlockSpec(memory_space=pltpu.SMEM)],
        out_specs=pl.BlockSpec(memory_space=pltpu.SMEM),
        compiler_params=pltpu.CompilerParams(vmem_limit_bytes=1 << 20),
        name="flag",
    )(pairs)


def plus_kernel(a, b, out):
    out[...] = a[...] + b[...]


def plus(a, b):
    return pl.pallas_call(
        plus_kernel,
        out_shape=pltpu.VMEM(a.shape, a.dtype),
        in_specs=[pl.BlockSpec(memory_space=pltpu.VMEM)] * 2,
        out_specs=pl.BlockSpec(memory_space=pltpu.VMEM),
        compiler_params=pltpu.CompilerParams(vmem_limit_bytes=1 << 20),
        name="plus",
    )(a, b)


def placed(owner_first, share, start, run, terms, total, scales=None):
    width = total.shape[1]
    columns = width // share * run
    part = terms[0][...]
    for term in terms[1:]:
        part = part + term[...]

    @pl.when(owner_first)
    def _():
        spread = jnp.concatenate(
            [part[:, n * columns : (n + 1) * columns] for n in range(share // run)], axis=0
        )
        lane = lax.broadcasted_iota(jnp.int32, (share, LANES), 1)
        for strip in range(width // share):
            source, target = strip * run, strip * share + start
            piece = spread[:, source // LANES * LANES : (source // LANES + 1) * LANES]
            shift = (target - source) % LANES
            if shift:
                piece = pltpu.roll(piece, shift, 1)
            tile = slice(target // LANES * LANES, (target // LANES + 1) * LANES)
            if scales is not None:
                piece = piece * scales[0][:, :1] * scales[1][:, tile]
            first = target % LANES
            inside = (lane >= first) & (lane < first + run)
            total[:, tile] = jnp.where(inside, piece, total[:, tile])

    @pl.when(jnp.logical_not(owner_first))
    def _():
        rows = part
        if scales is not None:
            rows = rows * scales[0][start : start + run, :1] * scales[1][...]
        total[start : start + run, :] = rows


def place_kernel(share, start, run, given, flag, *refs):
    *refs, total = refs
    owner_first = flag[0] == 1
    total[...] = refs[4][...] if given else jnp.zeros_like(total)
    placed(owner_first, share, start, run, refs[:4], total)
    if given > 1:
        total[...] = total[...] * refs[5][:, :1] * refs[6][...]


def scales_kernel(share, flag, norm_own, norm_low, rows, columns):
    width = columns.shape[1]
    owner_first = flag[0] == 1
    scale_own = lax.rsqrt(norm_own[...] + 1e-06)
    scale_low = lax.rsqrt(norm_low[...] + 1e-06)
    scale_first = jnp.where(owner_first, scale_own, scale_low)
    row = lax.broadcasted_iota(jnp.int32, (share, width), 0) + lax.axis_index("tm") * share
    column = lax.broadcasted_iota(jnp.int32, (share, width), 1)
    mine = jnp.sum(jnp.where(row == column, scale_first, 0.0), axis=1, keepdims=True)
    rows[...] = jnp.broadcast_to(mine, rows.shape)
    columns[...] = jnp.where(owner_first, scale_low, scale_own)


def finish_kernel(share, start, run, flag, base, rows, columns, *refs):
    *terms, out = refs
    owner_first = flag[0] == 1
    out[0] = base[...]
    placed(owner_first, share, start, run, terms, out.at[0], (rows, columns))


def small_call(kernel, out_shape, pairs, given, flops):
    return pl.pallas_call(
        kernel,
        out_shape=out_shape,
        in_specs=[pl.BlockSpec(memory_space=pltpu.SMEM)]
        + [pl.BlockSpec(memory_space=pltpu.VMEM)] * len(given),
        out_specs=jax.tree.map(lambda _: pl.BlockSpec(memory_space=pltpu.VMEM), out_shape),
        cost_estimate=pl.CostEstimate(
            flops=flops,
            bytes_accessed=sum(4 * x.size for x in given),
            transcendentals=0,
        ),
        compiler_params=pltpu.CompilerParams(vmem_limit_bytes=8 << 20),
    )(pairs, *given)


def place(pairs, terms, base, scales, share, width, start, run):
    given = [] if base is None else [base]
    given += list(scales)
    return small_call(
        functools.partial(place_kernel, share, start, run, len(given)),
        pltpu.VMEM((share, width), jnp.float32),
        pairs,
        list(terms) + given,
        2 * share * width * 256,
    )


def scales_of(pairs, norm_own, norm_low, share):
    width = norm_own.shape[1]
    return small_call(
        functools.partial(scales_kernel, share),
        (
            pltpu.VMEM((share, LANES), jnp.float32),
            pltpu.VMEM((1, width), jnp.float32),
        ),
        pairs,
        [norm_own, norm_low],
        share * width,
    )


def finish(pairs, base, scales, terms, share, start, run):
    return small_call(
        functools.partial(finish_kernel, share, start, run),
        jax.ShapeDtypeStruct((1,) + base.shape, jnp.float32),
        pairs,
        [base, *scales, *terms],
        2 * base.size * 256,
    )


def top_kernel(block, out, sems):
    step = out.shape[0] // TOPS
    copies = [
        pltpu.make_async_copy(
            block.at[pl.ds(n * step, step)], out.at[pl.ds(n * step, step)], sems.at[n]
        )
        for n in range(TOPS)
    ]
    for copy in copies:
        copy.start()
    for copy in copies:
        copy.wait()


def top_of(block, rows):
    return pl.pallas_call(
        top_kernel,
        out_shape=pltpu.VMEM((rows,) + block.shape[1:], block.dtype),
        in_specs=[pl.BlockSpec(memory_space=pltpu.HBM)],
        out_specs=pl.BlockSpec(memory_space=pltpu.VMEM),
        scratch_shapes=[pltpu.SemaphoreType.DMA((TOPS,))],
        compiler_params=pltpu.CompilerParams(vmem_limit_bytes=60 << 20),
        name="top",
    )(block)


def on_device(greens, pairs, onsets):
    rows_dev, width = greens.shape
    groups = lax.axis_size("tm")
    share = width // groups
    runs = runs_of(share)
    aligned = groups == 8 and all(
        run % 8 == 0
        and groups * run % LANES == 0
        and LANES % run == share % run == start % run == 0
        for start, run in runs
    )
    cut = rows_dev // HEAD

    head = from_behind(top_of(greens, cut), "src", 1)
    late = rows_dev - rows_dev // LATE
    pieces = [(cut, rows_dev, *run) for run in runs[:-1]]
    pieces += [(cut, late, *runs[-1]), (late, rows_dev, *runs[-1])]
    chosen = picks(greens, share, pieces)
    lower = []
    for block in chosen:
        lower.append(from_behind(block, "src", 1))
    own, squares = turn(onsets, greens)
    norm_own = summed(squares, "tm")
    norm_low = from_behind(norm_own, "src", 1)
    heads = picks(head, share, [(0, cut, *run) for run in runs])
    if not aligned:
        return plain_tail(pairs, own, heads, lower, norm_own[0], norm_low[0], share, runs)

    flag = flag_of(pairs)
    scales = scales_of(flag, norm_own, norm_low, share)
    base = None
    for step, (run, top) in enumerate(zip(runs, heads)):
        if step < len(runs) - 1:
            ranges, blocks = [(0, cut), (cut, rows_dev)], [top, lower[step]]
        else:
            so_far = early(own, [(0, cut), (cut, late)], [top, lower[-2]])
            ranges, blocks = [(late, rows_dev)], [lower[-1], so_far]
        keep, give = gram(flag, own, ranges, blocks, share, run[1])
        arrived = swapped(give, "tm", 1)
        mine, *gives = fold(keep, arrived)
        terms = [mine]
        for m, strip in enumerate(gives, 1):
            terms.append(swapped(strip, "tm", 2 * m))
        if step < len(runs) - 1:
            used = scales if step == len(runs) - 2 else ()
            base = place(flag, terms, base, used, share, width, *run)
    return finish(flag, base, scales, terms, share, *runs[-1])


def plain_tail(pairs, own, heads, lower, norm_own, norm_low, share, runs):
    row_group = lax.axis_index("tm")
    owner_first = pairs[0, 0] == lax.axis_index("src")
    flags = jnp.stack([owner_first.astype(jnp.int32), row_group % 2])
    parts = []
    rests = [[block] for block in lower[:-2]] + [lower[-2:]]
    for run, top, rest in zip(runs, heads, rests):
        keep, give = gram_plain(flags, own, [top, *rest], share, run[1])
        parts.append(functools.reduce(jnp.add, strips_arrived(keep, give, "tm")))
    scale_own = lax.rsqrt(norm_own + 1e-06)
    scale_low = lax.rsqrt(norm_low + 1e-06)
    scale_rows = lax.dynamic_slice_in_dim(
        jnp.where(owner_first, scale_own, scale_low), row_group * share, share, 0
    )[:, None]
    scale_cols = jnp.where(owner_first, scale_low, scale_own)[None, :]
    base = jnp.where(
        owner_first, put_back(runs, share, parts), jnp.concatenate(parts, axis=0)
    )
    return (base * scale_rows * scale_cols)[None]


def solution(mesh):
    in_specs = (P("tm", "src"), P("src", None), P())
    out_specs = P("src", "tm", None)
    return jax.shard_map(
        on_device, mesh=mesh, in_specs=in_specs, out_specs=out_specs, check_vma=False
    )
```
